32 devices in a mesh: rep: 2 (over y), tract: 4 (over x, core), head: 4 (over z).
Axes of the slice: x: 2, y: 2, z: 4, core: 2. Of those that a mesh axis runs over, the one named last changes fastest.
Arguments:
- frames: bfloat16 [8, 256, 6144], P(('rep', 'tract'), 'head'), parts along dimension 0, may hold values from -7 to 7
- levels: int32 [8], P(('rep', 'tract')), parts along dimension 0, may hold values from 0 to 7
- visible: int32 [8, 4], P(('rep', 'tract')), parts along dimension 0, may hold values from 0 to 1, as said below
- w_qkv: bfloat16 [6144, 3, 1024], P(None, None, 'head'), may hold values from -0.2 to 0.2
- w_out: bfloat16 [1024, 6144], P('head'), may hold values from -1.5 to 1.5
- modulation: float32 [8, 3, 6144], replicated, may hold values from -3 to 3
Outputs:
- mixed: bfloat16 [8, 256, 6144], P(('rep', 'tract'), 'head'), parts along dimension 0
The draws below stay inside these ranges and needn't reach their ends.
There are 2 independent parts, one for each index of `rep`. The reference program is written for one: setup_inputs(seed, part) draws one part's arguments, and reference() takes and returns one part's arrays. A program takes and returns all parts, laid end to end along the dimension named above; an argument that names none is the same for every part. Nothing has to cross between parts.
Inputs may be any that keep to these rules, and one draw needn't show every extreme that they name: visible[c, c] is 1 and visible[c, j] is 0 for every j > c.
All inputs are finite; a program needn't handle non-finite values.
Results may differ from the reference program's by a relative error of at most 0.019.
Values may be sent and summed in bfloat16 or wider, within the bound.
A program may use at most 64 MiB of HBM per device.

```python
import jax
import jax.numpy as jnp
from jax import lax

D = 6144
HD = 128
H_DEV = 2
CT = 256
NSTEP = 8
HEADS = 8
NCHUNK = 4
N_HEAD = 4


def draw_frames(key, part):
    base = jax.random.normal(jax.random.fold_in(key, 11), (NCHUNK, CT, D), jnp.float32)
    return jnp.clip(base, -6.5, 6.5).astype(jnp.bfloat16)


def draw_w_qkv(key, part):
    spread = D ** (-0.5)
    queries = spread * jax.random.normal(jax.random.fold_in(key, 21), (D, HEADS * HD), jnp.float32)
    key_part = spread * jax.random.normal(jax.random.fold_in(key, 22), (D, HEADS * HD), jnp.float32)
    values = spread * jax.random.normal(jax.random.fold_in(key, 23), (D, HEADS * HD), jnp.float32)
    stacked = jnp.stack([queries, key_part, values], axis=1)
    return jnp.clip(stacked, -0.19, 0.19).astype(jnp.bfloat16)


def draw_modulation(key, part):
    shift = 0.3 * jax.random.normal(jax.random.fold_in(key, 31), (NSTEP, D), jnp.float32)
    stretch = 0.3 * jax.random.normal(jax.random.fold_in(key, 32), (NSTEP, D), jnp.float32)
    gating = jax.random.normal(jax.random.fold_in(key, 33), (NSTEP, D), jnp.float32)
    return jnp.clip(jnp.stack([shift, stretch, gating], axis=1), -2.9, 2.9)


def draw_visible(key, part):
    coins = jax.random.randint(jax.random.fold_in(key, 41), (NCHUNK, NCHUNK), 0, 4)
    row_ids = jnp.arange(NCHUNK, dtype=jnp.int32)[:, None]
    col_ids = jnp.arange(NCHUNK, dtype=jnp.int32)[None, :]
    lower = jnp.where((coins > 0) & (row_ids > col_ids), 1, 0)
    return jnp.where(row_ids == col_ids, 1, lower).astype(jnp.int32)


def with_ends(result, rng, low, high):
    longest = result.shape.index(max(result.shape))
    spots = []
    for shift in (0, 1):
        where = [jax.random.randint(jax.random.fold_in(rng, axis), (), 0, length) for axis, length in enumerate(result.shape)]
        where[longest] = (where[longest] + shift) % result.shape[longest]
        spots.append(tuple(where))
    return result.at[spots[0]].set(low).at[spots[1]].set(high)


def block_scale(stream_key, dims, shards, least, top_value):
    gain = 1.0
    for dim, parts in shards:
        draws = jax.random.uniform(jax.random.fold_in(jax.random.fold_in(stream_key, 6), dim), (parts,), jnp.float32, least / len(shards), top_value / len(shards))
        gain = gain * jnp.repeat(jnp.exp(draws), dims[dim] // parts).reshape((-1,) + (1,) * (len(dims) - 1 - dim))
    return gain


def bell_draw(own_key, extent, deviation, bound, pieces=(), held_as=jnp.bfloat16):
    level = block_scale(own_key, extent, pieces, -0.22, 0.18) if pieces else 1.0
    array = jax.random.normal(own_key, extent, jnp.float32) * deviation * level
    return jnp.minimum(jnp.maximum(array, -bound), bound).astype(held_as)


def setup_inputs(seed: int = 0, part: int = 0) -> dict:
    splits = jax.random.split(jax.random.key(seed), 7)
    own_keys = jax.random.split(jax.random.fold_in(splits[6], part), 7)
    return {
        "frames": draw_frames(jax.random.fold_in(jax.random.fold_in(splits[6], part), 71), part),
        "levels": with_ends(jax.random.randint(own_keys[1], (NCHUNK,), 0, NSTEP), jax.random.fold_in(own_keys[1], 1), 0, NSTEP - 1).astype(jnp.int32),
        "visible": draw_visible(jax.random.fold_in(jax.random.fold_in(splits[6], part), 71), part),
        "w_qkv": draw_w_qkv(jax.random.fold_in(splits[6], 71), part),
        "w_out": bell_draw(splits[4], (HEADS * HD, D), (HEADS * HD // 64) ** -0.5, 1.5, ((0, 4),)),
        "modulation": draw_modulation(jax.random.fold_in(splits[6], 71), part),
    }


def reference(frames, levels, visible, w_qkv, w_out, modulation):
    styles = modulation[levels]
    floats = frames.astype(jnp.float32)
    normed = floats * lax.rsqrt(lax.optimization_barrier(jnp.mean(floats * floats, axis=-1, keepdims=True)) + 1e-06)
    shaped = (normed * (1.0 + styles[:, 1][:, None, :]) + styles[:, 0][:, None, :]).astype(jnp.bfloat16)
    qkv = jnp.dot(shaped.reshape(NCHUNK * CT, D), w_qkv.reshape(D, 3 * HEADS * HD), preferred_element_type=jnp.float32)
    qkv = qkv.astype(jnp.bfloat16).reshape(NCHUNK, CT, 3, HEADS, HD)
    queries = qkv[:, :, 0].astype(jnp.float32)
    key_rows = qkv[:, :, 1].astype(jnp.float32)
    values = qkv[:, :, 2].astype(jnp.float32)
    score_scale = HD ** (-0.5)

    def attend(inputs):
        query_block, visible_row = inputs
        scores = jnp.einsum('qhd,nkhd->qhnk', query_block, key_rows, precision=lax.Precision.HIGHEST) * score_scale
        allowed = (visible_row > 0)[None, None, :, None]
        scores = jnp.where(allowed, scores, -1e+30)
        row_peak = lax.optimization_barrier(jnp.max(scores, axis=(2, 3), keepdims=True))
        probs = jnp.where(allowed, jnp.exp(scores - row_peak), 0.0)
        denominator = lax.optimization_barrier(jnp.sum(probs, axis=(2, 3)))
        rounded = lax.optimization_barrier(probs.astype(jnp.bfloat16)).astype(jnp.float32)
        weighted = jnp.einsum('qhnk,nkhd->qhd', rounded, values, precision=lax.Precision.HIGHEST)
        return (weighted / denominator[:, :, None]).astype(jnp.bfloat16)
    attended = lax.map(attend, (queries, visible))
    flat = attended.reshape(NCHUNK * CT, HEADS * HD)
    span = H_DEV * HD

    def add_group(group, running):
        cols = lax.dynamic_slice_in_dim(flat, group * span, span, 1)
        rows = lax.dynamic_slice_in_dim(w_out, group * span, span, 0)
        partial_value = jnp.dot(cols, rows, preferred_element_type=jnp.float32)
        return running + lax.optimization_barrier(partial_value.astype(jnp.bfloat16)).astype(jnp.float32)
    summed = lax.fori_loop(0, N_HEAD, add_group, jnp.zeros((NCHUNK * CT, D), jnp.float32))
    summed = summed.reshape(NCHUNK, CT, D)
    return (summed * styles[:, 2][:, None, :]).astype(jnp.bfloat16)
```

```python
import functools

import jax
import jax.numpy as jnp
from jax import lax
from jax.experimental import pallas as pl
from jax.experimental.pallas import tpu as pltpu
from jax.sharding import PartitionSpec as P

HD = 128
MESH = pl.DeviceIdType.MESH


def meet(n, me):
    barrier = pltpu.get_barrier_semaphore()
    for other in (lax.rem(me + 1, n), lax.rem(me + n - 1, n)):
        pl.semaphore_signal(barrier, inc=1, device_id={"head": other}, device_id_type=MESH)
    pl.semaphore_wait(barrier, 2)


def gather_kernel(n, pieces, x_ref, out_ref, send_sem, recv_sem):
    me = lax.axis_index("head")
    meet(n, me)
    rows = x_ref.shape[1]
    step_rows = rows // pieces

    def copy(way, step, piece):
        block = me - way * step
        span = pl.ds(piece * step_rows, step_rows)
        return pltpu.make_async_remote_copy(
            src_ref=(x_ref.at[0] if step == 0 else out_ref.at[block]).at[span],
            dst_ref=out_ref.at[block].at[span],
            send_sem=send_sem.at[(way + 1) // 2, step, piece],
            recv_sem=recv_sem.at[(way + 1) // 2, step, piece],
            device_id={"head": me + way},
            device_id_type=MESH,
        )

    def arrival(way, step, piece):
        block = me - way * (step + 1)
        span = pl.ds(piece * step_rows, step_rows)
        return pltpu.make_async_remote_copy(
            src_ref=x_ref.at[0].at[span],
            dst_ref=out_ref.at[block].at[span],
            send_sem=send_sem.at[(way + 1) // 2, step, piece],
            recv_sem=recv_sem.at[(way + 1) // 2, step, piece],
            device_id={"head": me - way},
            device_id_type=MESH,
        )

    def sends(way, step):
        block, target = me - way * step, me + way
        return (block >= 0) & (block < n) & (target >= 0) & (target < n)

    def receives(way, step):
        block = me - way * (step + 1)
        return (block >= 0) & (block < n)

    for piece in range(pieces):
        for way in (-1, 1):

            @pl.when(sends(way, 0))
            def _():
                copy(way, 0, piece).start()

    out_ref[me] = x_ref[0]
    for step in range(n - 1):
        for piece in range(pieces):
            for way in (-1, 1):

                @pl.when(receives(way, step))
                def _():
                    arrival(way, step, piece).wait_recv()

                if step < n - 2:

                    @pl.when(sends(way, step + 1))
                    def _():
                        copy(way, step + 1, piece).start()

    for step in range(n - 1):
        for piece in range(pieces):
            for way in (-1, 1):

                @pl.when(sends(way, step))
                def _():
                    copy(way, step, piece).wait_send()


def gather_rows(frames, n):
    rows, width = frames.shape[1:]
    pieces = max(1, rows // 32)
    return pl.pallas_call(
        functools.partial(gather_kernel, n, pieces),
        out_shape=jax.ShapeDtypeStruct((n, rows, width), frames.dtype),
        in_specs=[pl.BlockSpec(memory_space=pltpu.VMEM)],
        out_specs=pl.BlockSpec(memory_space=pltpu.VMEM),
        scratch_shapes=[
            pltpu.SemaphoreType.DMA((2, n, pieces)),
            pltpu.SemaphoreType.DMA((2, n, pieces)),
        ],
        compiler_params=pltpu.CompilerParams(
            collective_id=0, has_side_effects=True, vmem_limit_bytes=24 << 20
        ),
    )(frames)


def scatter_kernel(n, pieces, a_ref, w_ref, out_ref, going, landed, send_sem, recv_sem):
    me = lax.axis_index("head")
    meet(n, me)
    rows = out_ref.shape[0]
    width = w_ref.shape[1]
    cols = width // pieces

    def copy(way, step, piece):
        side = (way + 1) // 2
        span = pl.ds(piece * cols, cols)
        return pltpu.make_async_remote_copy(
            src_ref=going.at[side, step].at[:, span],
            dst_ref=landed.at[side, step].at[:, span],
            send_sem=send_sem.at[side, step, piece],
            recv_sem=recv_sem.at[side, step, piece],
            device_id={"head": me + way},
            device_id_type=MESH,
        )

    def product(block, piece):
        return jnp.dot(
            a_ref[block],
            w_ref[:, piece * cols : (piece + 1) * cols],
            preferred_element_type=jnp.float32,
        )

    def owner(way, step):
        return (n - 1 - step) if way == 1 else step

    def sends(way, step):
        block = owner(way, step)
        return block > me if way == 1 else block < me

    def receives(way, step):
        block = owner(way, step)
        return (block >= me) & (me > 0) if way == 1 else (block <= me) & (me < n - 1)

    @pl.loop(0, n - 1)
    def _(tick):
        for piece in range(pieces):
            span = slice(piece * cols, (piece + 1) * cols)
            for way in (-1, 1):
                side = (way + 1) // 2
                step = tick - (me if way == 1 else n - 1 - me)
                held = (step >= 0) & (step < n - 1)

                @pl.when(held & sends(way, step))
                def _():
                    going[side, step, :, span] = product(owner(way, step), piece).astype(
                        going.dtype
                    )

                    @pl.when(receives(way, step))
                    def _():
                        copy(way, step, piece).wait_recv()
                        going[side, step, :, span] = (
                            going[side, step, :, span].astype(jnp.float32)
                            + landed[side, step, :, span].astype(jnp.float32)
                        ).astype(going.dtype)

                    copy(way, step, piece).start()

    for piece in range(pieces):
        span = slice(piece * cols, (piece + 1) * cols)
        out_ref[:, span] = product(me, piece).astype(going.dtype).astype(jnp.float32)
    for piece in range(pieces):
        span = slice(piece * cols, (piece + 1) * cols)
        for way in (-1, 1):
            side = (way + 1) // 2
            last = n - 1 - me if way == 1 else me

            @pl.when(last < n - 1)
            def _():
                copy(way, last, piece).wait_recv()
                out_ref[:, span] += landed[side, last, :, span].astype(jnp.float32)

    @pl.loop(0, n - 1)
    def _(step):
        for piece in range(pieces):
            for way in (-1, 1):

                @pl.when(sends(way, step))
                def _():
                    copy(way, step, piece).wait_send()


def scatter_sum(attended, w_out, n):
    total, depth = attended.shape
    rows, width = total // n, w_out.shape[1]
    pieces = 2 if rows >= 64 else 1
    return pl.pallas_call(
        functools.partial(scatter_kernel, n, pieces),
        out_shape=jax.ShapeDtypeStruct((rows, width), jnp.float32),
        in_specs=[pl.BlockSpec(memory_space=pltpu.VMEM)] * 2,
        out_specs=pl.BlockSpec(memory_space=pltpu.VMEM),
        scratch_shapes=[
            pltpu.VMEM((2, n - 1, rows, width), jnp.bfloat16),
            pltpu.VMEM((2, n - 1, rows, width), jnp.bfloat16),
            pltpu.SemaphoreType.DMA((2, n, pieces)),
            pltpu.SemaphoreType.DMA((2, n, pieces)),
        ],
        compiler_params=pltpu.CompilerParams(
            collective_id=1, has_side_effects=True, vmem_limit_bytes=40 << 20
        ),
    )(attended.reshape(n, rows, depth), w_out)


def from_behind(value, axis, by):
    count = lax.axis_size(axis)
    pairs = [(i, i + by) for i in range(count) if 0 <= i + by < count]
    return lax.ppermute(value, axis, pairs)


def body(frames, levels, visible, w_qkv, w_out, modulation):
    col_width = w_qkv.shape[2]
    heads_here = col_width // HD
    n_levels = modulation.shape[0]
    chosen = (lax.iota(jnp.int32, n_levels) == levels[0]).astype(jnp.float32)
    styles = jnp.tensordot(chosen, modulation, axes=1, precision=lax.Precision.HIGHEST)
    ranks = lax.axis_size("head")
    floats = gather_rows(frames, ranks).reshape(1, -1, frames.shape[2]).astype(jnp.float32)
    normed = floats * lax.rsqrt(jnp.mean(floats * floats, axis=-1, keepdims=True) + 1e-06)
    shaped = (normed * (1.0 + styles[1]) + styles[0]).astype(jnp.bfloat16)
    qkv = jnp.einsum("crd,dke->crke", shaped, w_qkv, preferred_element_type=jnp.float32).astype(
        jnp.bfloat16
    )
    total_rows = qkv.shape[1]
    queries = qkv[0, :, 0].reshape(total_rows, heads_here, HD)
    kv_block = qkv[:, :, 1:]
    visible_row = visible[0]
    score_scale = HD ** (-0.5)

    def absorb(state, incoming, offset):
        row_peak, denominator, running = state
        blocks = incoming.shape[0]
        allowed = (lax.dynamic_slice_in_dim(visible_row, offset, blocks) > 0) & (offset >= 0)
        key_rows = incoming[:, :, 0].reshape(blocks, total_rows, heads_here, HD)
        values = incoming[:, :, 1].reshape(blocks, total_rows, heads_here, HD)
        scores = (
            jnp.einsum("qhd,nkhd->qhnk", queries, key_rows, preferred_element_type=jnp.float32)
            * score_scale
        )
        allowed = allowed[None, None, :, None]
        scores = jnp.where(allowed, scores, -1e30)
        new_peak = jnp.maximum(row_peak, jnp.max(scores, axis=(2, 3)))
        probs = jnp.where(allowed, jnp.exp(scores - new_peak[:, :, None, None]), 0.0)
        rescale = jnp.exp(row_peak - new_peak)
        denominator = denominator * rescale + jnp.sum(probs, axis=(2, 3))
        weighted = jnp.einsum(
            "qhnk,nkhd->qhd", probs.astype(jnp.bfloat16), values, preferred_element_type=jnp.float32
        )
        running = running * rescale[:, :, None] + weighted
        return (new_peak, denominator, running)

    initial = (
        jnp.full((total_rows, heads_here), -1e30, jnp.float32),
        jnp.zeros((total_rows, heads_here), jnp.float32),
        jnp.zeros((total_rows, heads_here, HD), jnp.float32),
    )
    own_index = lax.axis_index("tract")
    state = absorb(initial, kv_block, own_index)
    for distance in range(1, lax.axis_size("tract")):
        moved = from_behind(kv_block, "tract", distance)
        state = absorb(state, moved, own_index - distance)
    row_peak, denominator, running = state
    attended = (
        (running / denominator[:, :, None]).astype(jnp.bfloat16).reshape(total_rows, col_width)
    )
    summed = scatter_sum(attended, w_out, ranks)
    mixed = (summed * styles[2]).astype(jnp.bfloat16)
    return mixed[None]


def solution(mesh):
    placed = (
        P(("rep", "tract"), "head", None),
        P(("rep", "tract")),
        P(("rep", "tract"), None),
        P(None, None, "head"),
        P("head", None),
        P(),
    )
    return jax.shard_map(
        body,
        mesh=mesh,
        in_specs=placed,
        out_specs=P(("rep", "tract"), "head", None),
        check_vma=False,
    )
```

```python
import functools

import jax
import jax.numpy as jnp
from jax import lax
from jax.experimental import pallas as pl
from jax.experimental.pallas import tpu as pltpu
from jax.sharding import PartitionSpec as P

HD = 128
MESH = pl.DeviceIdType.MESH


def meet(n, me):
    barrier = pltpu.get_barrier_semaphore()
    for other in (lax.rem(me + 1, n), lax.rem(me + n - 1, n)):
        pl.semaphore_signal(barrier, inc=1, device_id={"head": other}, device_id_type=MESH)
    pl.semaphore_wait(barrier, 2)


def project_kernel(
    n, pieces, x_ref, style_ref, w_hbm, q_ref, kv_ref, got, w_ref, w_sem, send_sem, recv_sem
):
    me = lax.axis_index("head")
    load = pltpu.make_async_copy(w_hbm, w_ref, w_sem)
    load.start()
    meet(n, me)
    rows, width = x_ref.shape[1:]
    part = rows // pieces

    def copy(way, step, piece, first=False):
        side = (way + 1) // 2
        span = pl.ds(piece * part, part)
        block = me - way * step
        return pltpu.make_async_remote_copy(
            src_ref=(x_ref.at[0] if first else got.at[block]).at[span],
            dst_ref=got.at[block].at[span],
            send_sem=send_sem.at[side, step, piece],
            recv_sem=recv_sem.at[side, step, piece],
            device_id={"head": me + way},
            device_id_type=MESH,
        )

    def arrival(way, step, piece):
        side = (way + 1) // 2
        span = pl.ds(piece * part, part)
        return pltpu.make_async_remote_copy(
            src_ref=x_ref.at[0].at[span],
            dst_ref=got.at[me - way * (step + 1)].at[span],
            send_sem=send_sem.at[side, step, piece],
            recv_sem=recv_sem.at[side, step, piece],
            device_id={"head": me - way},
            device_id_type=MESH,
        )

    def sends(way, step):
        block, target = me - way * step, me + way
        return (block >= 0) & (block < n) & (target >= 0) & (target < n) & (step < n - 1)

    def receives(way, step):
        block = me - way * (step + 1)
        return (block >= 0) & (block < n)

    def project(block):
        tokens = got[block].astype(jnp.float32)
        power = jnp.mean(tokens * tokens, axis=-1, keepdims=True)
        normed = tokens * lax.rsqrt(power + 1e-06)
        shaped = (normed * (1.0 + style_ref[1:2, :]) + style_ref[0:1, :]).astype(jnp.bfloat16)
        for kind in range(3):
            made = jnp.dot(shaped, w_ref[kind], preferred_element_type=jnp.float32)
            made = made.astype(jnp.bfloat16)
            if kind == 0:
                q_ref[block] = made
            else:
                kv_ref[kind - 1, block] = made

    for piece in range(pieces):
        for way in (-1, 1):

            @pl.when(sends(way, 0))
            def _():
                copy(way, 0, piece, True).start()

    got[me] = x_ref[0]
    load.wait()
    project(me)

    @pl.loop(0, n - 1)
    def _(step):
        for piece in range(pieces):
            for way in (-1, 1):

                @pl.when(receives(way, step))
                def _():
                    arrival(way, step, piece).wait_recv()

                @pl.when(sends(way, step + 1))
                def _():
                    copy(way, step + 1, piece).start()

        @pl.loop(0, 2)
        def _(side):
            way = 2 * side - 1

            @pl.when(receives(way, step))
            def _():
                project(me - way * (step + 1))

    @pl.loop(0, n - 1)
    def _(step):
        for piece in range(pieces):
            for way in (-1, 1):

                @pl.when(sends(way, step))
                def _():
                    copy(way, step, piece).wait_send()


def project_rows(frames, styles, w_qkv, n):
    rows, width = frames.shape[1:]
    cols = w_qkv.shape[2]
    pieces = max(1, rows // 32)
    vmem = pl.BlockSpec(memory_space=pltpu.VMEM)
    return pl.pallas_call(
        functools.partial(project_kernel, n, pieces),
        out_shape=(
            jax.ShapeDtypeStruct((n, rows, cols), frames.dtype),
            jax.ShapeDtypeStruct((2, n, rows, cols), frames.dtype),
        ),
        in_specs=[vmem, vmem, pl.BlockSpec(memory_space=pl.ANY)],
        out_specs=(vmem, vmem),
        scratch_shapes=[
            pltpu.VMEM((n, rows, width), frames.dtype),
            pltpu.VMEM((3, width, cols), w_qkv.dtype),
            pltpu.SemaphoreType.DMA,
            pltpu.SemaphoreType.DMA((2, n, pieces)),
            pltpu.SemaphoreType.DMA((2, n, pieces)),
        ],
        compiler_params=pltpu.CompilerParams(
            collective_id=0, has_side_effects=True, vmem_limit_bytes=36 << 20
        ),
    )(frames, styles, jnp.transpose(w_qkv, (1, 0, 2)))


def scatter_kernel(n, pieces, a_ref, w_ref, out_ref, going, landed, send_sem, recv_sem):
    me = lax.axis_index("head")
    meet(n, me)
    rows = out_ref.shape[0]
    width = w_ref.shape[1]
    cols = width // pieces

    def copy(way, step, piece):
        side = (way + 1) // 2
        span = pl.ds(piece * cols, cols)
        return pltpu.make_async_remote_copy(
            src_ref=going.at[side, step].at[:, span],
            dst_ref=landed.at[side, step].at[:, span],
            send_sem=send_sem.at[side, step, piece],
            recv_sem=recv_sem.at[side, step, piece],
            device_id={"head": me + way},
            device_id_type=MESH,
        )

    def product(block, piece):
        return jnp.dot(
            a_ref[block],
            w_ref[:, piece * cols : (piece + 1) * cols],
            preferred_element_type=jnp.float32,
        )

    def owner(way, step):
        return (n - 1 - step) if way == 1 else step

    def sends(way, step):
        block = owner(way, step)
        return block > me if way == 1 else block < me

    def receives(way, step):
        block = owner(way, step)
        return (block >= me) & (me > 0) if way == 1 else (block <= me) & (me < n - 1)

    @pl.loop(0, n - 1)
    def _(tick):
        for piece in range(pieces):
            span = slice(piece * cols, (piece + 1) * cols)
            for way in (-1, 1):
                side = (way + 1) // 2
                step = tick - (me if way == 1 else n - 1 - me)
                held = (step >= 0) & (step < n - 1)

                @pl.when(held & sends(way, step))
                def _():
                    going[side, step, :, span] = product(owner(way, step), piece).astype(
                        going.dtype
                    )

                    @pl.when(receives(way, step))
                    def _():
                        copy(way, step, piece).wait_recv()
                        going[side, step, :, span] = (
                            going[side, step, :, span].astype(jnp.float32)
                            + landed[side, step, :, span].astype(jnp.float32)
                        ).astype(going.dtype)

                    copy(way, step, piece).start()

    for piece in range(pieces):
        span = slice(piece * cols, (piece + 1) * cols)
        out_ref[:, span] = product(me, piece).astype(going.dtype).astype(jnp.float32)
    for piece in range(pieces):
        span = slice(piece * cols, (piece + 1) * cols)
        for way in (-1, 1):
            side = (way + 1) // 2
            last = n - 1 - me if way == 1 else me

            @pl.when(last < n - 1)
            def _():
                copy(way, last, piece).wait_recv()
                out_ref[:, span] += landed[side, last, :, span].astype(jnp.float32)

    @pl.loop(0, n - 1)
    def _(step):
        for piece in range(pieces):
            for way in (-1, 1):

                @pl.when(sends(way, step))
                def _():
                    copy(way, step, piece).wait_send()


def scatter_sum(attended, w_out, n):
    total, depth = attended.shape
    rows, width = total // n, w_out.shape[1]
    pieces = 2 if rows >= 64 else 1
    return pl.pallas_call(
        functools.partial(scatter_kernel, n, pieces),
        out_shape=jax.ShapeDtypeStruct((rows, width), jnp.float32),
        in_specs=[pl.BlockSpec(memory_space=pltpu.VMEM)] * 2,
        out_specs=pl.BlockSpec(memory_space=pltpu.VMEM),
        scratch_shapes=[
            pltpu.VMEM((2, n - 1, rows, width), jnp.bfloat16),
            pltpu.VMEM((2, n - 1, rows, width), jnp.bfloat16),
            pltpu.SemaphoreType.DMA((2, n, pieces)),
            pltpu.SemaphoreType.DMA((2, n, pieces)),
        ],
        compiler_params=pltpu.CompilerParams(
            collective_id=1, has_side_effects=True, vmem_limit_bytes=40 << 20
        ),
    )(attended.reshape(n, rows, depth), w_out)


def from_behind(value, axis, by):
    count = lax.axis_size(axis)
    pairs = [(i, i + by) for i in range(count) if 0 <= i + by < count]
    return lax.ppermute(value, axis, pairs)


def body(frames, levels, visible, w_qkv, w_out, modulation):
    col_width = w_qkv.shape[2]
    heads_here = col_width // HD
    n_levels = modulation.shape[0]
    chosen = (lax.iota(jnp.int32, n_levels) == levels[0]).astype(jnp.float32)
    styles = jnp.tensordot(chosen, modulation, axes=1, precision=lax.Precision.HIGHEST)
    ranks = lax.axis_size("head")
    queries, kv_block = project_rows(frames, styles, w_qkv, ranks)
    total_rows = queries.shape[0] * queries.shape[1]
    queries = queries.reshape(total_rows, heads_here, HD)
    kv_block = kv_block.reshape(1, 2, total_rows, col_width)
    visible_row = visible[0]
    score_scale = HD ** (-0.5)

    def absorb(state, incoming, offset):
        row_peak, denominator, running = state
        blocks = incoming.shape[0]
        allowed = (lax.dynamic_slice_in_dim(visible_row, offset, blocks) > 0) & (offset >= 0)
        key_rows = incoming[:, 0].reshape(blocks, total_rows, heads_here, HD)
        values = incoming[:, 1].reshape(blocks, total_rows, heads_here, HD)
        scores = (
            jnp.einsum("qhd,nkhd->qhnk", queries, key_rows, preferred_element_type=jnp.float32)
            * score_scale
        )
        allowed = allowed[None, None, :, None]
        scores = jnp.where(allowed, scores, -1e30)
        new_peak = jnp.maximum(row_peak, jnp.max(scores, axis=(2, 3)))
        probs = jnp.where(allowed, jnp.exp(scores - new_peak[:, :, None, None]), 0.0)
        rescale = jnp.exp(row_peak - new_peak)
        denominator = denominator * rescale + jnp.sum(probs, axis=(2, 3))
        weighted = jnp.einsum(
            "qhnk,nkhd->qhd", probs.astype(jnp.bfloat16), values, preferred_element_type=jnp.float32
        )
        running = running * rescale[:, :, None] + weighted
        return (new_peak, denominator, running)

    initial = (
        jnp.full((total_rows, heads_here), -1e30, jnp.float32),
        jnp.zeros((total_rows, heads_here), jnp.float32),
        jnp.zeros((total_rows, heads_here, HD), jnp.float32),
    )
    own_index = lax.axis_index("tract")
    state = absorb(initial, kv_block, own_index)
    for distance in range(1, lax.axis_size("tract")):
        moved = from_behind(kv_block, "tract", distance)
        state = absorb(state, moved, own_index - distance)
    row_peak, denominator, running = state
    attended = (
        (running / denominator[:, :, None]).astype(jnp.bfloat16).reshape(total_rows, col_width)
    )
    summed = scatter_sum(attended, w_out, ranks)
    mixed = (summed * styles[2]).astype(jnp.bfloat16)
    return mixed[None]


def solution(mesh):
    placed = (
        P(("rep", "tract"), "head", None),
        P(("rep", "tract")),
        P(("rep", "tract"), None),
        P(None, None, "head"),
        P("head", None),
        P(),
    )
    return jax.shard_map(
        body,
        mesh=mesh,
        in_specs=placed,
        out_specs=P(("rep", "tract"), "head", None),
        check_vma=False,
    )
```

```python
import functools

import jax
import jax.numpy as jnp
from jax import lax
from jax.experimental import pallas as pl
from jax.experimental.pallas import tpu as pltpu
from jax.sharding import PartitionSpec as P

HD = 128
GRANT = 60 * 1024 * 1024
MESH = pl.DeviceIdType.MESH


def meet(n, me):
    barrier = pltpu.get_barrier_semaphore()
    for other in (lax.rem(me + 1, n), lax.rem(me + n - 1, n)):
        pl.semaphore_signal(barrier, inc=1, device_id={"head": other}, device_id_type=MESH)
    pl.semaphore_wait(barrier, 2)


def project_kernel(
    n, pieces, x_ref, style_ref, w_hbm, q_ref, kv_ref, got, w_ref, w_sem, send_sem, recv_sem
):
    me = lax.axis_index("head")
    own = pltpu.make_async_copy(x_ref.at[0], got.at[me], w_sem.at[0])
    own.start()
    load = pltpu.make_async_copy(w_hbm, w_ref, w_sem.at[1])
    load.start()
    meet(n, me)
    rows, width = x_ref.shape[1:]
    part = rows // pieces

    def copy(way, step, piece, first=False):
        side = (way + 1) // 2
        span = pl.ds(piece * part, part)
        block = me - way * step
        return pltpu.make_async_remote_copy(
            src_ref=(x_ref.at[0] if first else got.at[block]).at[span],
            dst_ref=got.at[block].at[span],
            send_sem=send_sem.at[side, step, piece],
            recv_sem=recv_sem.at[side, step, piece],
            device_id={"head": me + way},
            device_id_type=MESH,
        )

    def arrival(way, step, piece):
        side = (way + 1) // 2
        span = pl.ds(piece * part, part)
        return pltpu.make_async_remote_copy(
            src_ref=x_ref.at[0].at[span],
            dst_ref=got.at[me - way * (step + 1)].at[span],
            send_sem=send_sem.at[side, step, piece],
            recv_sem=recv_sem.at[side, step, piece],
            device_id={"head": me - way},
            device_id_type=MESH,
        )

    def sends(way, step):
        block, target = me - way * step, me + way
        return (block >= 0) & (block < n) & (target >= 0) & (target < n) & (step < n - 1)

    def receives(way, step):
        block = me - way * (step + 1)
        return (block >= 0) & (block < n)

    def project(block):
        tokens = got[block].astype(jnp.float32)
        power = jnp.mean(tokens * tokens, axis=-1, keepdims=True)
        normed = tokens * lax.rsqrt(power + 1e-06)
        shaped = (normed * (1.0 + style_ref[1:2, :]) + style_ref[0:1, :]).astype(jnp.bfloat16)
        for kind in range(3):
            made = jnp.dot(shaped, w_ref[kind], preferred_element_type=jnp.float32)
            made = made.astype(jnp.bfloat16)
            if kind == 0:
                q_ref[block] = made
            else:
                kv_ref[kind - 1, block] = made

    for piece in range(pieces):
        for way in (-1, 1):

            @pl.when(sends(way, 0))
            def _():
                copy(way, 0, piece, True).start()

    own.wait()
    load.wait()
    project(me)

    @pl.loop(0, n - 1)
    def _(step):
        for piece in range(pieces):
            for way in (-1, 1):

                @pl.when(receives(way, step))
                def _():
                    arrival(way, step, piece).wait_recv()

                @pl.when(sends(way, step + 1))
                def _():
                    copy(way, step + 1, piece).start()

        @pl.loop(0, 2)
        def _(side):
            way = 2 * side - 1

            @pl.when(receives(way, step))
            def _():
                project(me - way * (step + 1))

    @pl.loop(0, n - 1)
    def _(step):
        for piece in range(pieces):
            for way in (-1, 1):

                @pl.when(sends(way, step))
                def _():
                    copy(way, step, piece).wait_send()


def project_rows(frames, styles, w_qkv, n):
    rows, width = frames.shape[1:]
    cols = w_qkv.shape[2]
    pieces = max(1, rows // 32)
    vmem = pl.BlockSpec(memory_space=pltpu.VMEM)
    hbm = pl.BlockSpec(memory_space=pltpu.HBM)
    return pl.pallas_call(
        functools.partial(project_kernel, n, pieces),
        out_shape=(
            jax.ShapeDtypeStruct((n, rows, cols), frames.dtype),
            jax.ShapeDtypeStruct((2, n, rows, cols), frames.dtype),
        ),
        in_specs=[hbm, vmem, hbm],
        out_specs=(vmem, vmem),
        scratch_shapes=[
            pltpu.VMEM((n, rows, width), frames.dtype),
            pltpu.VMEM((3, width, cols), w_qkv.dtype),
            pltpu.SemaphoreType.DMA((2,)),
            pltpu.SemaphoreType.DMA((2, n, pieces)),
            pltpu.SemaphoreType.DMA((2, n, pieces)),
        ],
        compiler_params=pltpu.CompilerParams(
            collective_id=0, has_side_effects=True, vmem_limit_bytes=GRANT
        ),
    )(frames, styles, jnp.transpose(w_qkv, (1, 0, 2)))


def scatter_kernel(
    n, pieces, a_ref, w_hbm, out_ref, w_ref, going, landed, w_sem, send_sem, recv_sem
):
    me = lax.axis_index("head")
    load = pltpu.make_async_copy(w_hbm, w_ref, w_sem)
    load.start()
    meet(n, me)
    load.wait()
    rows = out_ref.shape[0]
    width = w_ref.shape[1]
    cols = width // pieces

    def copy(way, step, piece):
        side = (way + 1) // 2
        span = pl.ds(piece * cols, cols)
        return pltpu.make_async_remote_copy(
            src_ref=going.at[side, step].at[:, span],
            dst_ref=landed.at[side, step].at[:, span],
            send_sem=send_sem.at[side, step, piece],
            recv_sem=recv_sem.at[side, step, piece],
            device_id={"head": me + way},
            device_id_type=MESH,
        )

    def product(block, piece):
        return jnp.dot(
            a_ref[block],
            w_ref[:, piece * cols : (piece + 1) * cols],
            preferred_element_type=jnp.float32,
        )

    def owner(way, step):
        return (n - 1 - step) if way == 1 else step

    def sends(way, step):
        block = owner(way, step)
        return block > me if way == 1 else block < me

    def receives(way, step):
        block = owner(way, step)
        return (block >= me) & (me > 0) if way == 1 else (block <= me) & (me < n - 1)

    @pl.loop(0, n - 1)
    def _(tick):
        for piece in range(pieces):
            span = slice(piece * cols, (piece + 1) * cols)
            for way in (-1, 1):
                side = (way + 1) // 2
                step = tick - (me if way == 1 else n - 1 - me)
                held = (step >= 0) & (step < n - 1)

                @pl.when(held & sends(way, step))
                def _():
                    going[side, step, :, span] = product(owner(way, step), piece).astype(
                        going.dtype
                    )

                    @pl.when(receives(way, step))
                    def _():
                        copy(way, step, piece).wait_recv()
                        going[side, step, :, span] = (
                            going[side, step, :, span].astype(jnp.float32)
                            + landed[side, step, :, span].astype(jnp.float32)
                        ).astype(going.dtype)

                    copy(way, step, piece).start()

    for piece in range(pieces):
        span = slice(piece * cols, (piece + 1) * cols)
        out_ref[:, span] = product(me, piece).astype(going.dtype).astype(jnp.float32)
    for piece in range(pieces):
        span = slice(piece * cols, (piece + 1) * cols)
        for way in (-1, 1):
            side = (way + 1) // 2
            last = n - 1 - me if way == 1 else me

            @pl.when(last < n - 1)
            def _():
                copy(way, last, piece).wait_recv()
                out_ref[:, span] += landed[side, last, :, span].astype(jnp.float32)

    @pl.loop(0, n - 1)
    def _(step):
        for piece in range(pieces):
            for way in (-1, 1):

                @pl.when(sends(way, step))
                def _():
                    copy(way, step, piece).wait_send()


def scatter_sum(attended, w_out, n):
    total, depth = attended.shape
    rows, width = total // n, w_out.shape[1]
    pieces = 2 if rows >= 64 else 1
    return pl.pallas_call(
        functools.partial(scatter_kernel, n, pieces),
        out_shape=jax.ShapeDtypeStruct((rows, width), jnp.float32),
        in_specs=[
            pl.BlockSpec(memory_space=pltpu.VMEM),
            pl.BlockSpec(memory_space=pltpu.HBM),
        ],
        out_specs=pl.BlockSpec(memory_space=pltpu.VMEM),
        scratch_shapes=[
            pltpu.VMEM(w_out.shape, w_out.dtype),
            pltpu.VMEM((2, n - 1, rows, width), jnp.bfloat16),
            pltpu.VMEM((2, n - 1, rows, width), jnp.bfloat16),
            pltpu.SemaphoreType.DMA,
            pltpu.SemaphoreType.DMA((2, n, pieces)),
            pltpu.SemaphoreType.DMA((2, n, pieces)),
        ],
        compiler_params=pltpu.CompilerParams(
            collective_id=1, has_side_effects=True, vmem_limit_bytes=GRANT
        ),
    )(attended.reshape(n, rows, depth), w_out)


def from_behind(value, axis, by):
    count = lax.axis_size(axis)
    pairs = [(i, i + by) for i in range(count) if 0 <= i + by < count]
    return lax.ppermute(value, axis, pairs)


def body(frames, levels, visible, w_qkv, w_out, modulation):
    col_width = w_qkv.shape[2]
    heads_here = col_width // HD
    n_levels = modulation.shape[0]
    chosen = (lax.iota(jnp.int32, n_levels) == levels[0]).astype(jnp.float32)
    styles = jnp.tensordot(chosen, modulation, axes=1, precision=lax.Precision.HIGHEST)
    ranks = lax.axis_size("head")
    queries, kv_block = project_rows(frames, styles, w_qkv, ranks)
    total_rows = queries.shape[0] * queries.shape[1]
    queries = queries.reshape(total_rows, heads_here, HD)
    kv_block = kv_block.reshape(1, 2, total_rows, col_width)
    visible_row = visible[0]
    score_scale = HD ** (-0.5)

    def absorb(state, incoming, offset):
        row_peak, denominator, running = state
        blocks = incoming.shape[0]
        allowed = (lax.dynamic_slice_in_dim(visible_row, offset, blocks) > 0) & (offset >= 0)
        key_rows = incoming[:, 0].reshape(blocks, total_rows, heads_here, HD)
        values = incoming[:, 1].reshape(blocks, total_rows, heads_here, HD)
        scores = (
            jnp.einsum("qhd,nkhd->qhnk", queries, key_rows, preferred_element_type=jnp.float32)
            * score_scale
        )
        allowed = allowed[None, None, :, None]
        scores = jnp.where(allowed, scores, -1e30)
        new_peak = jnp.maximum(row_peak, jnp.max(scores, axis=(2, 3)))
        probs = jnp.where(allowed, jnp.exp(scores - new_peak[:, :, None, None]), 0.0)
        rescale = jnp.exp(row_peak - new_peak)
        denominator = denominator * rescale + jnp.sum(probs, axis=(2, 3))
        weighted = jnp.einsum(
            "qhnk,nkhd->qhd", probs.astype(jnp.bfloat16), values, preferred_element_type=jnp.float32
        )
        running = running * rescale[:, :, None] + weighted
        return (new_peak, denominator, running)

    initial = (
        jnp.full((total_rows, heads_here), -1e30, jnp.float32),
        jnp.zeros((total_rows, heads_here), jnp.float32),
        jnp.zeros((total_rows, heads_here, HD), jnp.float32),
    )
    own_index = lax.axis_index("tract")
    state = absorb(initial, kv_block, own_index)
    for distance in range(1, lax.axis_size("tract")):
        moved = from_behind(kv_block, "tract", distance)
        state = absorb(state, moved, own_index - distance)
    row_peak, denominator, running = state
    attended = (
        (running / denominator[:, :, None]).astype(jnp.bfloat16).reshape(total_rows, col_width)
    )
    summed = scatter_sum(attended, w_out, ranks)
    mixed = (summed * styles[2]).astype(jnp.bfloat16)
    return mixed[None]


def solution(mesh):
    placed = (
        P(("rep", "tract"), "head", None),
        P(("rep", "tract")),
        P(("rep", "tract"), None),
        P(None, None, "head"),
        P("head", None),
        P(),
    )
    return jax.shard_map(
        body,
        mesh=mesh,
        in_specs=placed,
        out_specs=P(("rep", "tract"), "head", None),
        check_vma=False,
    )
```

```python
import functools

import jax
import jax.numpy as jnp
from jax import lax
from jax.experimental import pallas as pl
from jax.experimental.pallas import tpu as pltpu
from jax.sharding import PartitionSpec as P

HD = 128
GRANT = 60 * 1024 * 1024
MESH = pl.DeviceIdType.MESH


def meet(n, me, tracts, tract):
    barrier = pltpu.get_barrier_semaphore()
    for other in (lax.rem(me + 1, n), lax.rem(me + n - 1, n)):
        pl.semaphore_signal(barrier, inc=1, device_id={"head": other}, device_id_type=MESH)
    for ahead in range(1, tracts):
        other = lax.rem(tract + ahead, tracts)
        pl.semaphore_signal(barrier, inc=1, device_id={"tract": other}, device_id_type=MESH)
    pl.semaphore_wait(barrier, 1 + tracts)


def sublayer_kernel(
    n,
    tracts,
    pieces,
    halves,
    x_ref,
    level_ref,
    visible_ref,
    w_hbm,
    out_hbm,
    table_ref,
    out_ref,
    got,
    wq_ref,
    w_ref,
    q_ref,
    kv_ref,
    kv_in,
    att_ref,
    peak_ref,
    sum_ref,
    acc_ref,
    going,
    landed,
    total_ref,
    load_sem,
    g_send,
    g_recv,
    kv_send,
    kv_recv,
    s_send,
    s_recv,
):
    me, tract = lax.axis_index("head"), lax.axis_index("tract")
    own = pltpu.make_async_copy(x_ref.at[0], got.at[me], load_sem.at[0])
    own.start()
    load = pltpu.make_async_copy(w_hbm, wq_ref, load_sem.at[1])
    load.start()
    load_out = pltpu.make_async_copy(out_hbm, w_ref, load_sem.at[2])
    load_out.start()
    meet(n, me, tracts, tract)
    level = level_ref[0]

    def style(kind):
        return table_ref[kind, pl.ds(level, 1), :]

    rows, width = x_ref.shape[1:]
    part = rows // pieces

    def copy(way, step, piece, first=False):
        side = (way + 1) // 2
        span = pl.ds(piece * part, part)
        block = me - way * step
        return pltpu.make_async_remote_copy(
            src_ref=(x_ref.at[0] if first else got.at[block]).at[span],
            dst_ref=got.at[block].at[span],
            send_sem=g_send.at[side, step, piece],
            recv_sem=g_recv.at[side, step, piece],
            device_id={"head": me + way},
            device_id_type=MESH,
        )

    def arrival(way, step, piece):
        side = (way + 1) // 2
        span = pl.ds(piece * part, part)
        return pltpu.make_async_remote_copy(
            src_ref=x_ref.at[0].at[span],
            dst_ref=got.at[me - way * (step + 1)].at[span],
            send_sem=g_send.at[side, step, piece],
            recv_sem=g_recv.at[side, step, piece],
            device_id={"head": me - way},
            device_id_type=MESH,
        )

    def sends(way, step):
        block, target = me - way * step, me + way
        return (block >= 0) & (block < n) & (target >= 0) & (target < n) & (step < n - 1)

    def receives(way, step):
        block = me - way * (step + 1)
        return (block >= 0) & (block < n)

    def kv_copy(ahead, block):
        return pltpu.make_async_remote_copy(
            src_ref=kv_ref.at[block],
            dst_ref=kv_in.at[ahead - 1, block],
            send_sem=kv_send.at[ahead - 1, block],
            recv_sem=kv_recv.at[ahead - 1, block],
            device_id={"tract": tract + ahead},
            device_id_type=MESH,
        )

    def project(block):
        tokens = got[block].astype(jnp.float32)
        power = jnp.mean(tokens * tokens, axis=-1, keepdims=True)
        normed = tokens * lax.rsqrt(power + 1e-06)
        shaped = (normed * (1.0 + style(1)) + style(0)).astype(jnp.bfloat16)
        for kind in (1, 2, 0):
            made = jnp.dot(shaped, wq_ref[kind], preferred_element_type=jnp.float32)
            made = made.astype(jnp.bfloat16)
            if kind == 0:
                q_ref[block] = made
            else:
                kv_ref[block, kind - 1] = made
            if kind == 2:
                for ahead in range(1, tracts):

                    @pl.when(tract + ahead < tracts)
                    def _():
                        kv_copy(ahead, block).start()

    for piece in range(pieces):
        for way in (-1, 1):

            @pl.when(sends(way, 0))
            def _():
                copy(way, 0, piece, True).start()

    own.wait()
    load.wait()
    project(me)

    @pl.loop(0, n - 1)
    def _(step):
        for piece in range(pieces):
            for way in (-1, 1):

                @pl.when(receives(way, step))
                def _():
                    arrival(way, step, piece).wait_recv()

                @pl.when(sends(way, step + 1))
                def _():
                    copy(way, step + 1, piece).start()

        @pl.loop(0, 2)
        def _(side):
            way = 2 * side - 1

            @pl.when(receives(way, step))
            def _():
                project(me - way * (step + 1))

    @pl.loop(0, n - 1)
    def _(step):
        for piece in range(pieces):
            for way in (-1, 1):

                @pl.when(sends(way, step))
                def _():
                    copy(way, step, piece).wait_send()

    tokens_here = n * rows
    heads_here = q_ref.shape[2] // HD
    scale = HD ** (-0.5)

    def attend(source, allowed):
        for head in range(heads_here):
            lanes = slice(head * HD, (head + 1) * HD)
            queries = q_ref[:, :, lanes].reshape(tokens_here, HD)
            keys = source[:, 0, :, lanes].reshape(tokens_here, HD)
            values = source[:, 1, :, lanes].reshape(tokens_here, HD)
            scores = (
                lax.dot_general(
                    queries, keys, (((1,), (1,)), ((), ())), preferred_element_type=jnp.float32
                )
                * scale
            )
            if allowed is None:
                peak = jnp.max(scores, axis=1, keepdims=True)
                probs = jnp.exp(scores - peak)
            else:
                scores = jnp.where(allowed, scores, -1e30)
                old = peak_ref[head]
                peak = jnp.maximum(old, jnp.max(scores, axis=1, keepdims=True))
                probs = jnp.where(allowed, jnp.exp(scores - peak), 0.0)
                rescale = jnp.exp(old - peak)
            row_sum = jnp.sum(probs, axis=1, keepdims=True)
            weighted = jnp.dot(
                probs.astype(jnp.bfloat16), values, preferred_element_type=jnp.float32
            )
            if allowed is not None:
                row_sum += sum_ref[head] * rescale
                weighted += acc_ref[head] * rescale
            peak_ref[head] = peak
            sum_ref[head] = row_sum
            acc_ref[head] = weighted

    attend(kv_ref, None)
    for ahead in range(1, tracts):

        @pl.when(tract >= ahead)
        def _():
            @pl.loop(0, n)
            def _(block):
                kv_copy(ahead, block).wait_recv()

            attend(kv_in.at[ahead - 1], visible_ref[0, lax.max(tract - ahead, 0)] > 0)

    for head in range(heads_here):
        attended = (acc_ref[head] / sum_ref[head]).astype(jnp.bfloat16)
        att_ref[:, :, head * HD : (head + 1) * HD] = attended.reshape(n, rows, HD)
    load_out.wait()
    cols = width // halves

    def sum_copy(way, step, piece):
        side = (way + 1) // 2
        span = pl.ds(piece * cols, cols)
        return pltpu.make_async_remote_copy(
            src_ref=going.at[side, step].at[:, span],
            dst_ref=landed.at[side, step].at[:, span],
            send_sem=s_send.at[side, step, piece],
            recv_sem=s_recv.at[side, step, piece],
            device_id={"head": me + way},
            device_id_type=MESH,
        )

    def product(block, piece):
        return jnp.dot(
            att_ref[block],
            w_ref[:, piece * cols : (piece + 1) * cols],
            preferred_element_type=jnp.float32,
        )

    def owner(way, step):
        return (n - 1 - step) if way == 1 else step

    def sum_sends(way, step):
        block = owner(way, step)
        return block > me if way == 1 else block < me

    def sum_receives(way, step):
        block = owner(way, step)
        return (block >= me) & (me > 0) if way == 1 else (block <= me) & (me < n - 1)

    @pl.loop(0, n - 1)
    def _(tick):
        for piece in range(halves):
            span = slice(piece * cols, (piece + 1) * cols)
            for way in (-1, 1):
                side = (way + 1) // 2
                step = tick - (me if way == 1 else n - 1 - me)
                held = (step >= 0) & (step < n - 1)

                @pl.when(held & sum_sends(way, step))
                def _():
                    going[side, step, :, span] = product(owner(way, step), piece).astype(
                        going.dtype
                    )

                    @pl.when(sum_receives(way, step))
                    def _():
                        sum_copy(way, step, piece).wait_recv()
                        going[side, step, :, span] = (
                            going[side, step, :, span].astype(jnp.float32)
                            + landed[side, step, :, span].astype(jnp.float32)
                        ).astype(going.dtype)

                    sum_copy(way, step, piece).start()

    for piece in range(halves):
        span = slice(piece * cols, (piece + 1) * cols)
        total_ref[:, span] = product(me, piece).astype(going.dtype).astype(jnp.float32)
    for piece in range(halves):
        span = slice(piece * cols, (piece + 1) * cols)
        for way in (-1, 1):
            side = (way + 1) // 2
            last = n - 1 - me if way == 1 else me

            @pl.when(last < n - 1)
            def _():
                sum_copy(way, last, piece).wait_recv()
                total_ref[:, span] += landed[side, last, :, span].astype(jnp.float32)

        out_ref[0, :, span] = (
            total_ref[:, span] * table_ref[2, pl.ds(level, 1), span]
        ).astype(out_ref.dtype)

    @pl.loop(0, n - 1)
    def _(step):
        for piece in range(halves):
            for way in (-1, 1):

                @pl.when(sum_sends(way, step))
                def _():
                    sum_copy(way, step, piece).wait_send()

    @pl.loop(0, n)
    def _(block):
        for ahead in range(1, tracts):

            @pl.when(tract + ahead < tracts)
            def _():
                kv_copy(ahead, block).wait_send()


def body(frames, levels, visible, w_qkv, w_out, modulation):
    n, tracts = lax.axis_size("head"), lax.axis_size("tract")
    rows, width = frames.shape[1:]
    cols = w_qkv.shape[2]
    heads_here = cols // HD
    pieces = max(1, rows // 32)
    halves = 2
    vmem = pl.BlockSpec(memory_space=pltpu.VMEM)
    hbm = pl.BlockSpec(memory_space=pltpu.HBM)
    smem = pl.BlockSpec(memory_space=pltpu.SMEM)
    half = jnp.bfloat16
    dma = pltpu.SemaphoreType.DMA
    return pl.pallas_call(
        functools.partial(sublayer_kernel, n, tracts, pieces, halves),
        out_shape=jax.ShapeDtypeStruct(frames.shape, frames.dtype),
        in_specs=[hbm, smem, smem, hbm, hbm, vmem],
        out_specs=vmem,
        scratch_shapes=[
            pltpu.VMEM((n, rows, width), half),
            pltpu.VMEM((3, width, cols), half),
            pltpu.VMEM(w_out.shape, half),
            pltpu.VMEM((n, rows, cols), half),
            pltpu.VMEM((n, 2, rows, cols), half),
            pltpu.VMEM((max(1, tracts - 1), n, 2, rows, cols), half),
            pltpu.VMEM((n, rows, cols), half),
            pltpu.VMEM((heads_here, n * rows, 1), jnp.float32),
            pltpu.VMEM((heads_here, n * rows, 1), jnp.float32),
            pltpu.VMEM((heads_here, n * rows, HD), jnp.float32),
            pltpu.VMEM((2, n - 1, rows, width), half),
            pltpu.VMEM((2, n - 1, rows, width), half),
            pltpu.VMEM((rows, width), jnp.float32),
            dma((3,)),
            dma((2, n, pieces)),
            dma((2, n, pieces)),
            dma((tracts, n)),
            dma((tracts, n)),
            dma((2, n, halves)),
            dma((2, n, halves)),
        ],
        compiler_params=pltpu.CompilerParams(
            collective_id=0, has_side_effects=True, vmem_limit_bytes=GRANT
        ),
    )(
        frames,
        levels,
        visible,
        jnp.transpose(w_qkv, (1, 0, 2)),
        w_out,
        jnp.transpose(modulation, (1, 0, 2)),
    )


def solution(mesh):
    placed = (
        P(("rep", "tract"), "head", None),
        P(("rep", "tract")),
        P(("rep", "tract"), None),
        P(None, None, "head"),
        P("head", None),
        P(),
    )
    return jax.shard_map(
        body,
        mesh=mesh,
        in_specs=placed,
        out_specs=P(("rep", "tract"), "head", None),
        check_vma=False,
    )
```

```python
import functools

import jax
import jax.numpy as jnp
from jax import lax
from jax.experimental import pallas as pl
from jax.experimental.pallas import tpu as pltpu
from jax.sharding import PartitionSpec as P

HD = 128
GRANT = 60 * 1024 * 1024
MESH = pl.DeviceIdType.MESH


def meet(n, me, tracts, tract, others):
    barrier = pltpu.get_barrier_semaphore()
    for other in (lax.rem(me + 1, n), lax.rem(me + n - 1, n)):
        pl.semaphore_signal(barrier, inc=1, device_id={"head": other}, device_id_type=MESH)
    for ahead in range(1, tracts):
        other = lax.rem(tract + ahead, tracts)
        pl.semaphore_signal(barrier, inc=1, device_id={"tract": other}, device_id_type=MESH)
    for other in others:
        pl.semaphore_signal(barrier, inc=1, device_id=other, device_id_type=MESH)
    pl.semaphore_wait(barrier, 1 + tracts + len(others))


def sublayer_kernel(
    n,
    tracts,
    reps,
    pieces,
    halves,
    x_ref,
    level_ref,
    visible_ref,
    w_hbm,
    out_hbm,
    table_ref,
    out_ref,
    got,
    wq_ref,
    w_ref,
    q_ref,
    kv_ref,
    kv_in,
    att_ref,
    peak_ref,
    sum_ref,
    acc_ref,
    going,
    landed,
    total_ref,
    load_sem,
    g_send,
    g_recv,
    kv_send,
    kv_recv,
    s_send,
    s_recv,
    w_far,
    att_far,
    f_send,
    f_recv,
):
    me, tract = lax.axis_index("head"), lax.axis_index("tract")
    own = pltpu.make_async_copy(x_ref.at[0], got.at[me], load_sem.at[0])
    own.start()
    load = pltpu.make_async_copy(w_hbm, wq_ref, load_sem.at[1])
    load.start()
    load_out = pltpu.make_async_copy(out_hbm, w_ref, load_sem.at[2])
    load_out.start()
    core, wide = tract % 2, tracts // 2
    chips = wide * reps
    chip = lax.axis_index("rep") * wide + tract // 2
    slab = w_ref.shape[0] // (2 * chips)
    helper = (me == 1) | (me == n - 2)
    ends = (me == 0) | (me == n - 1)

    def seat(by):
        other = lax.rem(chip + by, chips)
        return {"rep": other // wide, "tract": lax.rem(other, wide) * 2 + core}

    def slab_of(which, side):
        start = pl.multiple_of((which * 2 + side) * slab, slab)
        return pl.ds(start, slab)

    def far_copy(kind, span, target, source=None):
        return pltpu.make_async_remote_copy(
            src_ref=(w_far if source is None else source).at[span],
            dst_ref=w_far.at[span],
            send_sem=f_send.at[kind],
            recv_sem=f_recv.at[kind],
            device_id=target,
            device_id_type=MESH,
        )

    inward = {"head": jnp.where(me == 0, 1, n - 2)}
    partner = {"tract": tract + 1 - 2 * core}
    mine = slab_of(chip, core)

    def to_helper():
        return far_copy(0, mine, inward, out_hbm)

    def to_chip(by):
        return far_copy(by, mine, seat(by))

    def from_chip(by):
        return far_copy(by, slab_of(lax.rem(chip + chips - by, chips), core), seat(by))

    def to_partner(by):
        span = slab_of(lax.rem(chip + chips - by, chips), core)
        return far_copy(chips + by, span, partner)

    def from_partner(by):
        span = slab_of(lax.rem(chip + chips - by, chips), 1 - core)
        return far_copy(chips + by, span, partner)

    def att_copy():
        return pltpu.make_async_remote_copy(
            src_ref=att_ref,
            dst_ref=att_far,
            send_sem=f_send.at[2 * chips],
            recv_sem=f_recv.at[2 * chips],
            device_id=inward,
            device_id_type=MESH,
        )

    meet(n, me, tracts, tract, [seat(by) for by in range(1, chips)])
    level = level_ref[0]

    def style(kind):
        return table_ref[kind, pl.ds(level, 1), :]

    rows, width = x_ref.shape[1:]
    part = rows // pieces

    def copy(way, step, piece, first=False):
        side = (way + 1) // 2
        span = pl.ds(piece * part, part)
        block = me - way * step
        return pltpu.make_async_remote_copy(
            src_ref=(x_ref.at[0] if first else got.at[block]).at[span],
            dst_ref=got.at[block].at[span],
            send_sem=g_send.at[side, step, piece],
            recv_sem=g_recv.at[side, step, piece],
            device_id={"head": me + way},
            device_id_type=MESH,
        )

    def arrival(way, step, piece):
        side = (way + 1) // 2
        span = pl.ds(piece * part, part)
        return pltpu.make_async_remote_copy(
            src_ref=x_ref.at[0].at[span],
            dst_ref=got.at[me - way * (step + 1)].at[span],
            send_sem=g_send.at[side, step, piece],
            recv_sem=g_recv.at[side, step, piece],
            device_id={"head": me - way},
            device_id_type=MESH,
        )

    def sends(way, step):
        block, target = me - way * step, me + way
        return (block >= 0) & (block < n) & (target >= 0) & (target < n) & (step < n - 1)

    def receives(way, step):
        block = me - way * (step + 1)
        return (block >= 0) & (block < n)

    def kv_copy(ahead, block):
        return pltpu.make_async_remote_copy(
            src_ref=kv_ref.at[block],
            dst_ref=kv_in.at[ahead - 1, block],
            send_sem=kv_send.at[ahead - 1, block],
            recv_sem=kv_recv.at[ahead - 1, block],
            device_id={"tract": tract + ahead},
            device_id_type=MESH,
        )

    def project(block):
        tokens = got[block].astype(jnp.float32)
        power = jnp.mean(tokens * tokens, axis=-1, keepdims=True)
        normed = tokens * lax.rsqrt(power + 1e-06)
        shaped = (normed * (1.0 + style(1)) + style(0)).astype(jnp.bfloat16)
        for kind in (1, 2, 0):
            made = jnp.dot(shaped, wq_ref[kind], preferred_element_type=jnp.float32)
            made = made.astype(jnp.bfloat16)
            if kind == 0:
                q_ref[block] = made
            else:
                kv_ref[block, kind - 1] = made
            if kind == 2:
                for ahead in range(1, tracts):

                    @pl.when(tract + ahead < tracts)
                    def _():
                        kv_copy(ahead, block).start()

    for piece in range(pieces):
        for way in (-1, 1):

            @pl.when(sends(way, 0))
            def _():
                copy(way, 0, piece, True).start()

    @pl.when(ends)
    def _():
        to_helper().start()

    own.wait()
    load.wait()
    project(me)

    @pl.loop(0, n - 1)
    def _(step):
        for piece in range(pieces):
            for way in (-1, 1):

                @pl.when(receives(way, step))
                def _():
                    arrival(way, step, piece).wait_recv()

                @pl.when(sends(way, step + 1))
                def _():
                    copy(way, step + 1, piece).start()

        @pl.loop(0, 2)
        def _(side):
            way = 2 * side - 1

            @pl.when(receives(way, step))
            def _():
                project(me - way * (step + 1))

        @pl.when(helper & (step == 0))
        def _():
            to_helper().wait_recv()
            for by in range(1, chips):
                to_chip(by).start()
            to_partner(0).start()

    @pl.when(helper)
    def _():
        for by in range(1, chips):
            from_chip(by).wait_recv()
            to_partner(by).start()

    @pl.loop(0, n - 1)
    def _(step):
        for piece in range(pieces):
            for way in (-1, 1):

                @pl.when(sends(way, step))
                def _():
                    copy(way, step, piece).wait_send()

    tokens_here = n * rows
    heads_here = q_ref.shape[2] // HD
    scale = HD ** (-0.5)

    def attend(source, allowed):
        for head in range(heads_here):
            lanes = slice(head * HD, (head + 1) * HD)
            queries = q_ref[:, :, lanes].reshape(tokens_here, HD)
            keys = source[:, 0, :, lanes].reshape(tokens_here, HD)
            values = source[:, 1, :, lanes].reshape(tokens_here, HD)
            scores = (
                lax.dot_general(
                    queries, keys, (((1,), (1,)), ((), ())), preferred_element_type=jnp.float32
                )
                * scale
            )
            if allowed is None:
                peak = jnp.max(scores, axis=1, keepdims=True)
                probs = jnp.exp(scores - peak)
            else:
                scores = jnp.where(allowed, scores, -1e30)
                old = peak_ref[head]
                peak = jnp.maximum(old, jnp.max(scores, axis=1, keepdims=True))
                probs = jnp.where(allowed, jnp.exp(scores - peak), 0.0)
                rescale = jnp.exp(old - peak)
            row_sum = jnp.sum(probs, axis=1, keepdims=True)
            weighted = jnp.dot(
                probs.astype(jnp.bfloat16), values, preferred_element_type=jnp.float32
            )
            if allowed is not None:
                row_sum += sum_ref[head] * rescale
                weighted += acc_ref[head] * rescale
            peak_ref[head] = peak
            sum_ref[head] = row_sum
            acc_ref[head] = weighted

    attend(kv_ref, None)
    for ahead in range(1, tracts):

        @pl.when(tract >= ahead)
        def _():
            @pl.loop(0, n)
            def _(block):
                kv_copy(ahead, block).wait_recv()

            attend(kv_in.at[ahead - 1], visible_ref[0, lax.max(tract - ahead, 0)] > 0)

    for head in range(heads_here):
        attended = (acc_ref[head] / sum_ref[head]).astype(jnp.bfloat16)
        att_ref[:, :, head * HD : (head + 1) * HD] = attended.reshape(n, rows, HD)

    @pl.when(ends)
    def _():
        att_copy().start()

    load_out.wait()

    @pl.when(helper)
    def _():
        for by in range(chips):
            from_partner(by).wait_recv()
        att_copy().wait_recv()

    cols = width // halves

    def sum_copy(way, step, piece):
        side = (way + 1) // 2
        span = pl.ds(piece * cols, cols)
        return pltpu.make_async_remote_copy(
            src_ref=going.at[side, step].at[:, span],
            dst_ref=landed.at[side, step].at[:, span],
            send_sem=s_send.at[side, step, piece],
            recv_sem=s_recv.at[side, step, piece],
            device_id={"head": me + way},
            device_id_type=MESH,
        )

    def product(block, piece):
        return jnp.dot(
            att_ref[block],
            w_ref[:, piece * cols : (piece + 1) * cols],
            preferred_element_type=jnp.float32,
        )

    def far_product(block, piece):
        return jnp.dot(
            att_far[block],
            w_far[:, piece * cols : (piece + 1) * cols],
            preferred_element_type=jnp.float32,
        )

    def helps(way):
        return me == (1 if way == 1 else n - 2)

    def owner(way, step):
        return (n - 1 - step) if way == 1 else step

    def sum_sends(way, step):
        block = owner(way, step)
        return (block > me) & (me > 0) if way == 1 else (block < me) & (me < n - 1)

    def sum_receives(way, step):
        block = owner(way, step)
        return (block >= me) & (me > 1) if way == 1 else (block <= me) & (me < n - 2)

    @pl.loop(0, n - 1)
    def _(tick):
        for piece in range(halves):
            span = slice(piece * cols, (piece + 1) * cols)
            for way in (-1, 1):
                side = (way + 1) // 2
                step = tick - (me if way == 1 else n - 1 - me)
                held = (step >= 0) & (step < n - 1)

                @pl.when(held & sum_sends(way, step))
                def _():
                    going[side, step, :, span] = product(owner(way, step), piece).astype(
                        going.dtype
                    )

                    @pl.when(helps(way))
                    def _():
                        going[side, step, :, span] = (
                            going[side, step, :, span].astype(jnp.float32)
                            + far_product(owner(way, step), piece)
                        ).astype(going.dtype)

                    @pl.when(sum_receives(way, step))
                    def _():
                        sum_copy(way, step, piece).wait_recv()
                        going[side, step, :, span] = (
                            going[side, step, :, span].astype(jnp.float32)
                            + landed[side, step, :, span].astype(jnp.float32)
                        ).astype(going.dtype)

                    sum_copy(way, step, piece).start()

    for piece in range(halves):
        span = slice(piece * cols, (piece + 1) * cols)
        total_ref[:, span] = product(me, piece).astype(going.dtype).astype(jnp.float32)
    for piece in range(halves):
        span = slice(piece * cols, (piece + 1) * cols)
        for way in (-1, 1):
            side = (way + 1) // 2
            last = n - 1 - me if way == 1 else me

            @pl.when(helps(way))
            def _():
                total_ref[:, span] += far_product(me, piece)

            @pl.when(me > 1 if way == 1 else me < n - 2)
            def _():
                sum_copy(way, last, piece).wait_recv()
                total_ref[:, span] += landed[side, last, :, span].astype(jnp.float32)

        out_ref[0, :, span] = (
            total_ref[:, span] * table_ref[2, pl.ds(level, 1), span]
        ).astype(out_ref.dtype)

    @pl.loop(0, n - 1)
    def _(step):
        for piece in range(halves):
            for way in (-1, 1):

                @pl.when(sum_sends(way, step))
                def _():
                    sum_copy(way, step, piece).wait_send()

    @pl.loop(0, n)
    def _(block):
        for ahead in range(1, tracts):

            @pl.when(tract + ahead < tracts)
            def _():
                kv_copy(ahead, block).wait_send()

    @pl.when(ends)
    def _():
        to_helper().wait_send()
        att_copy().wait_send()

    @pl.when(helper)
    def _():
        for by in range(1, chips):
            to_chip(by).wait_send()
        for by in range(chips):
            to_partner(by).wait_send()


def body(frames, levels, visible, w_qkv, w_out, modulation):
    n, tracts = lax.axis_size("head"), lax.axis_size("tract")
    reps = lax.axis_size("rep")
    rows, width = frames.shape[1:]
    cols = w_qkv.shape[2]
    heads_here = cols // HD
    pieces = max(1, rows // 32)
    halves = 2
    vmem = pl.BlockSpec(memory_space=pltpu.VMEM)
    hbm = pl.BlockSpec(memory_space=pltpu.HBM)
    smem = pl.BlockSpec(memory_space=pltpu.SMEM)
    half = jnp.bfloat16
    dma = pltpu.SemaphoreType.DMA
    return pl.pallas_call(
        functools.partial(sublayer_kernel, n, tracts, reps, pieces, halves),
        out_shape=jax.ShapeDtypeStruct(frames.shape, frames.dtype),
        in_specs=[hbm, smem, smem, hbm, hbm, vmem],
        out_specs=vmem,
        scratch_shapes=[
            pltpu.VMEM((n, rows, width), half),
            pltpu.VMEM((3, width, cols), half),
            pltpu.VMEM(w_out.shape, half),
            pltpu.VMEM((n, rows, cols), half),
            pltpu.VMEM((n, 2, rows, cols), half),
            pltpu.VMEM((max(1, tracts - 1), n, 2, rows, cols), half),
            pltpu.VMEM((n, rows, cols), half),
            pltpu.VMEM((heads_here, n * rows, 1), jnp.float32),
            pltpu.VMEM((heads_here, n * rows, 1), jnp.float32),
            pltpu.VMEM((heads_here, n * rows, HD), jnp.float32),
            pltpu.VMEM((2, n - 1, rows, width), half),
            pltpu.VMEM((2, n - 1, rows, width), half),
            pltpu.VMEM((rows, width), jnp.float32),
            dma((3,)),
            dma((2, n, pieces)),
            dma((2, n, pieces)),
            dma((tracts, n)),
            dma((tracts, n)),
            dma((2, n, halves)),
            dma((2, n, halves)),
            pltpu.VMEM(w_out.shape, half),
            pltpu.VMEM((n, rows, cols), half),
            dma((tracts * reps + 1,)),
            dma((tracts * reps + 1,)),
        ],
        compiler_params=pltpu.CompilerParams(
            collective_id=0, has_side_effects=True, vmem_limit_bytes=GRANT
        ),
    )(
        frames,
        levels,
        visible,
        jnp.transpose(w_qkv, (1, 0, 2)),
        w_out,
        jnp.transpose(modulation, (1, 0, 2)),
    )


def solution(mesh):
    placed = (
        P(("rep", "tract"), "head", None),
        P(("rep", "tract")),
        P(("rep", "tract"), None),
        P(None, None, "head"),
        P("head", None),
        P(),
    )
    return jax.shard_map(
        body,
        mesh=mesh,
        in_specs=placed,
        out_specs=P(("rep", "tract"), "head", None),
        check_vma=False,
    )
```

```python
import functools

import jax
import jax.numpy as jnp
from jax import lax
from jax.experimental import pallas as pl
from jax.experimental.pallas import tpu as pltpu
from jax.sharding import PartitionSpec as P

HD = 128
GRANT = 60 * 1024 * 1024
MESH = pl.DeviceIdType.MESH


def meet(n, me, tracts, tract, others):
    barrier = pltpu.get_barrier_semaphore()
    for other in (lax.rem(me + 1, n), lax.rem(me + n - 1, n)):
        pl.semaphore_signal(barrier, inc=1, device_id={"head": other}, device_id_type=MESH)
    for ahead in range(1, tracts):
        other = lax.rem(tract + ahead, tracts)
        pl.semaphore_signal(barrier, inc=1, device_id={"tract": other}, device_id_type=MESH)
    for other in others:
        pl.semaphore_signal(barrier, inc=1, device_id=other, device_id_type=MESH)
    pl.semaphore_wait(barrier, 1 + tracts + len(others))


def sublayer_kernel(
    n,
    tracts,
    reps,
    pieces,
    halves,
    x_ref,
    level_ref,
    visible_ref,
    w_hbm,
    out_hbm,
    table_ref,
    out_ref,
    got,
    wq_ref,
    w_ref,
    q_ref,
    kv_ref,
    kv_in,
    att_ref,
    peak_ref,
    sum_ref,
    acc_ref,
    going,
    landed,
    total_ref,
    load_sem,
    g_send,
    g_recv,
    kv_send,
    kv_recv,
    s_send,
    s_recv,
    w_far,
    att_far,
    f_send,
    f_recv,
):
    me, tract = lax.axis_index("head"), lax.axis_index("tract")
    own = pltpu.make_async_copy(x_ref.at[0], got.at[me], load_sem.at[0])
    own.start()
    load = pltpu.make_async_copy(w_hbm, wq_ref, load_sem.at[1])
    load.start()
    load_out = pltpu.make_async_copy(out_hbm, w_ref, load_sem.at[2])
    load_out.start()
    core, wide = tract % 2, tracts // 2
    chips = wide * reps
    chip = lax.axis_index("rep") * wide + tract // 2
    slab = w_ref.shape[0] // (2 * chips)
    helper = (me == 1) | (me == n - 2)
    ends = (me == 0) | (me == n - 1)

    def seat(by):
        other = lax.rem(chip + by, chips)
        return {"rep": other // wide, "tract": lax.rem(other, wide) * 2 + core}

    def slab_of(which, side):
        start = pl.multiple_of((which * 2 + side) * slab, slab)
        return pl.ds(start, slab)

    def far_copy(kind, span, target, source=None):
        return pltpu.make_async_remote_copy(
            src_ref=(w_far if source is None else source).at[span],
            dst_ref=w_far.at[span],
            send_sem=f_send.at[kind],
            recv_sem=f_recv.at[kind],
            device_id=target,
            device_id_type=MESH,
        )

    inward = {"head": jnp.where(me == 0, 1, n - 2)}
    partner = {"tract": tract + 1 - 2 * core}
    mine = slab_of(chip, core)

    def to_helper():
        return far_copy(0, mine, inward, out_hbm)

    def to_chip(by):
        return far_copy(by, mine, seat(by))

    def from_chip(by):
        return far_copy(by, slab_of(lax.rem(chip + chips - by, chips), core), seat(by))

    def to_partner(by):
        span = slab_of(lax.rem(chip + chips - by, chips), core)
        return far_copy(chips + by, span, partner)

    def from_partner(by):
        span = slab_of(lax.rem(chip + chips - by, chips), 1 - core)
        return far_copy(chips + by, span, partner)

    def att_copy():
        return pltpu.make_async_remote_copy(
            src_ref=att_ref,
            dst_ref=att_far,
            send_sem=f_send.at[2 * chips],
            recv_sem=f_recv.at[2 * chips],
            device_id=inward,
            device_id_type=MESH,
        )

    meet(n, me, tracts, tract, [seat(by) for by in range(1, chips)])
    level = level_ref[0]

    def style(kind):
        return table_ref[kind, pl.ds(level, 1), :]

    rows, width = x_ref.shape[1:]
    part = rows // pieces

    def copy(way, step, piece, first=False):
        side = (way + 1) // 2
        span = pl.ds(piece * part, part)
        block = me - way * step
        return pltpu.make_async_remote_copy(
            src_ref=(x_ref.at[0] if first else got.at[block]).at[span],
            dst_ref=got.at[block].at[span],
            send_sem=g_send.at[side, step, piece],
            recv_sem=g_recv.at[side, step, piece],
            device_id={"head": me + way},
            device_id_type=MESH,
        )

    def arrival(way, step, piece):
        side = (way + 1) // 2
        span = pl.ds(piece * part, part)
        return pltpu.make_async_remote_copy(
            src_ref=x_ref.at[0].at[span],
            dst_ref=got.at[me - way * (step + 1)].at[span],
            send_sem=g_send.at[side, step, piece],
            recv_sem=g_recv.at[side, step, piece],
            device_id={"head": me - way},
            device_id_type=MESH,
        )

    def sends(way, step):
        block, target = me - way * step, me + way
        return (block >= 0) & (block < n) & (target >= 0) & (target < n) & (step < n - 1)

    def receives(way, step):
        block = me - way * (step + 1)
        return (block >= 0) & (block < n)

    def kv_copy(ahead, block):
        return pltpu.make_async_remote_copy(
            src_ref=kv_ref.at[block],
            dst_ref=kv_in.at[ahead - 1, block],
            send_sem=kv_send.at[ahead - 1, block],
            recv_sem=kv_recv.at[ahead - 1, block],
            device_id={"tract": tract + ahead},
            device_id_type=MESH,
        )

    def project(block):
        tokens = got[block].astype(jnp.float32)
        power = jnp.mean(tokens * tokens, axis=-1, keepdims=True)
        normed = tokens * lax.rsqrt(power + 1e-06)
        shaped = (normed * (1.0 + style(1)) + style(0)).astype(jnp.bfloat16)
        for kind in (1, 2, 0):
            made = jnp.dot(shaped, wq_ref[kind], preferred_element_type=jnp.float32)
            made = made.astype(jnp.bfloat16)
            if kind == 0:
                q_ref[block] = made
            else:
                kv_ref[block, kind - 1] = made
            if kind == 2:
                for ahead in range(1, tracts):

                    @pl.when(tract + ahead < tracts)
                    def _():
                        kv_copy(ahead, block).start()

    for piece in range(pieces):
        for way in (-1, 1):

            @pl.when(sends(way, 0))
            def _():
                copy(way, 0, piece, True).start()

    @pl.when(ends)
    def _():
        to_helper().start()

    own.wait()
    load.wait()
    project(me)

    @pl.loop(0, n - 1)
    def _(step):
        for piece in range(pieces):
            for way in (-1, 1):

                @pl.when(receives(way, step))
                def _():
                    arrival(way, step, piece).wait_recv()

                @pl.when(sends(way, step + 1))
                def _():
                    copy(way, step + 1, piece).start()

        @pl.loop(0, 2)
        def _(side):
            way = 2 * side - 1

            @pl.when(receives(way, step))
            def _():
                project(me - way * (step + 1))

        @pl.when(helper & (step == 0))
        def _():
            to_helper().wait_recv()
            for by in range(1, chips):
                to_chip(by).start()
            to_partner(0).start()

    @pl.when(helper)
    def _():
        for by in range(1, chips):
            from_chip(by).wait_recv()
            to_partner(by).start()

    tokens_here = n * rows
    heads_here = q_ref.shape[2] // HD
    scale = HD ** (-0.5)

    def attend(source, allowed):
        for head in range(heads_here):
            lanes = slice(head * HD, (head + 1) * HD)
            queries = q_ref[:, :, lanes].reshape(tokens_here, HD)
            keys = source[:, 0, :, lanes].reshape(tokens_here, HD)
            values = source[:, 1, :, lanes].reshape(tokens_here, HD)
            scores = (
                lax.dot_general(
                    queries, keys, (((1,), (1,)), ((), ())), preferred_element_type=jnp.float32
                )
                * scale
            )
            if allowed is None:
                peak = jnp.max(scores, axis=1, keepdims=True)
                probs = jnp.exp(scores - peak)
            else:
                scores = jnp.where(allowed, scores, -1e30)
                old = peak_ref[head]
                peak = jnp.maximum(old, jnp.max(scores, axis=1, keepdims=True))
                probs = jnp.where(allowed, jnp.exp(scores - peak), 0.0)
                rescale = jnp.exp(old - peak)
            row_sum = jnp.sum(probs, axis=1, keepdims=True)
            weighted = jnp.dot(
                probs.astype(jnp.bfloat16), values, preferred_element_type=jnp.float32
            )
            if allowed is not None:
                row_sum += sum_ref[head] * rescale
                weighted += acc_ref[head] * rescale
            peak_ref[head] = peak
            sum_ref[head] = row_sum
            acc_ref[head] = weighted

    attend(kv_ref, None)
    for ahead in range(1, tracts):

        @pl.when(tract >= ahead)
        def _():
            @pl.loop(0, n)
            def _(block):
                kv_copy(ahead, block).wait_recv()

            attend(kv_in.at[ahead - 1], visible_ref[0, lax.max(tract - ahead, 0)] > 0)

    for head in range(heads_here):
        attended = (acc_ref[head] / sum_ref[head]).astype(jnp.bfloat16)
        att_ref[:, :, head * HD : (head + 1) * HD] = attended.reshape(n, rows, HD)

    @pl.when(ends)
    def _():
        att_copy().start()

    load_out.wait()

    @pl.when(helper)
    def _():
        for by in range(chips):
            from_partner(by).wait_recv()
        att_copy().wait_recv()

    cols = width // halves

    def sum_copy(way, step, piece):
        side = (way + 1) // 2
        span = pl.ds(piece * cols, cols)
        return pltpu.make_async_remote_copy(
            src_ref=going.at[side, step].at[:, span],
            dst_ref=landed.at[side, step].at[:, span],
            send_sem=s_send.at[side, step, piece],
            recv_sem=s_recv.at[side, step, piece],
            device_id={"head": me + way},
            device_id_type=MESH,
        )

    def product(block, piece):
        return jnp.dot(
            att_ref[block],
            w_ref[:, piece * cols : (piece + 1) * cols],
            preferred_element_type=jnp.float32,
        )

    def far_product(block, piece):
        return jnp.dot(
            att_far[block],
            w_far[:, piece * cols : (piece + 1) * cols],
            preferred_element_type=jnp.float32,
        )

    def helps(way):
        return me == (1 if way == 1 else n - 2)

    def owner(way, step):
        return (n - 1 - step) if way == 1 else step

    def sum_sends(way, step):
        block = owner(way, step)
        return (block > me) & (me > 0) if way == 1 else (block < me) & (me < n - 1)

    def sum_receives(way, step):
        block = owner(way, step)
        return (block >= me) & (me > 1) if way == 1 else (block <= me) & (me < n - 2)

    @pl.loop(0, n - 1)
    def _(tick):
        for piece in range(halves):
            span = slice(piece * cols, (piece + 1) * cols)
            for way in (-1, 1):
                side = (way + 1) // 2
                step = tick - (me if way == 1 else n - 1 - me)
                held = (step >= 0) & (step < n - 1)

                @pl.when(held & sum_sends(way, step))
                def _():
                    going[side, step, :, span] = product(owner(way, step), piece).astype(
                        going.dtype
                    )

                    @pl.when(helps(way))
                    def _():
                        going[side, step, :, span] = (
                            going[side, step, :, span].astype(jnp.float32)
                            + far_product(owner(way, step), piece)
                        ).astype(going.dtype)

                    @pl.when(sum_receives(way, step))
                    def _():
                        sum_copy(way, step, piece).wait_recv()
                        going[side, step, :, span] = (
                            going[side, step, :, span].astype(jnp.float32)
                            + landed[side, step, :, span].astype(jnp.float32)
                        ).astype(going.dtype)

                    sum_copy(way, step, piece).start()

    for piece in range(halves):
        span = slice(piece * cols, (piece + 1) * cols)
        total_ref[:, span] = product(me, piece).astype(going.dtype).astype(jnp.float32)
    for piece in range(halves):
        span = slice(piece * cols, (piece + 1) * cols)
        for way in (-1, 1):
            side = (way + 1) // 2
            last = n - 1 - me if way == 1 else me

            @pl.when(helps(way))
            def _():
                total_ref[:, span] += far_product(me, piece)

            @pl.when(me > 1 if way == 1 else me < n - 2)
            def _():
                sum_copy(way, last, piece).wait_recv()
                total_ref[:, span] += landed[side, last, :, span].astype(jnp.float32)

        out_ref[0, :, span] = (
            total_ref[:, span] * table_ref[2, pl.ds(level, 1), span]
        ).astype(out_ref.dtype)

    @pl.loop(0, n - 1)
    def _(step):
        for piece in range(halves):
            for way in (-1, 1):

                @pl.when(sum_sends(way, step))
                def _():
                    sum_copy(way, step, piece).wait_send()

    @pl.loop(0, n)
    def _(block):
        for ahead in range(1, tracts):

            @pl.when(tract + ahead < tracts)
            def _():
                kv_copy(ahead, block).wait_send()

    @pl.loop(0, n - 1)
    def _(step):
        for piece in range(pieces):
            for way in (-1, 1):

                @pl.when(sends(way, step))
                def _():
                    copy(way, step, piece).wait_send()

    @pl.when(ends)
    def _():
        to_helper().wait_send()
        att_copy().wait_send()

    @pl.when(helper)
    def _():
        for by in range(1, chips):
            to_chip(by).wait_send()
        for by in range(chips):
            to_partner(by).wait_send()


def body(frames, levels, visible, w_qkv, w_out, modulation):
    n, tracts = lax.axis_size("head"), lax.axis_size("tract")
    reps = lax.axis_size("rep")
    rows, width = frames.shape[1:]
    cols = w_qkv.shape[2]
    heads_here = cols // HD
    pieces = max(1, rows // 32)
    halves = 4 if width % 512 == 0 else 2
    vmem = pl.BlockSpec(memory_space=pltpu.VMEM)
    hbm = pl.BlockSpec(memory_space=pltpu.HBM)
    smem = pl.BlockSpec(memory_space=pltpu.SMEM)
    half = jnp.bfloat16
    dma = pltpu.SemaphoreType.DMA
    return pl.pallas_call(
        functools.partial(sublayer_kernel, n, tracts, reps, pieces, halves),
        out_shape=jax.ShapeDtypeStruct(frames.shape, frames.dtype),
        in_specs=[hbm, smem, smem, hbm, hbm, vmem],
        out_specs=vmem,
        scratch_shapes=[
            pltpu.VMEM((n, rows, width), half),
            pltpu.VMEM((3, width, cols), half),
            pltpu.VMEM(w_out.shape, half),
            pltpu.VMEM((n, rows, cols), half),
            pltpu.VMEM((n, 2, rows, cols), half),
            pltpu.VMEM((max(1, tracts - 1), n, 2, rows, cols), half),
            pltpu.VMEM((n, rows, cols), half),
            pltpu.VMEM((heads_here, n * rows, 1), jnp.float32),
            pltpu.VMEM((heads_here, n * rows, 1), jnp.float32),
            pltpu.VMEM((heads_here, n * rows, HD), jnp.float32),
            pltpu.VMEM((2, n - 1, rows, width), half),
            pltpu.VMEM((2, n - 1, rows, width), half),
            pltpu.VMEM((rows, width), jnp.float32),
            dma((3,)),
            dma((2, n, pieces)),
            dma((2, n, pieces)),
            dma((tracts, n)),
            dma((tracts, n)),
            dma((2, n, halves)),
            dma((2, n, halves)),
            pltpu.VMEM(w_out.shape, half),
            pltpu.VMEM((n, rows, cols), half),
            dma((tracts * reps + 1,)),
            dma((tracts * reps + 1,)),
        ],
        compiler_params=pltpu.CompilerParams(
            collective_id=0, has_side_effects=True, vmem_limit_bytes=GRANT
        ),
    )(
        frames,
        levels,
        visible,
        jnp.transpose(w_qkv, (1, 0, 2)),
        w_out,
        jnp.transpose(modulation, (1, 0, 2)),
    )


def solution(mesh):
    placed = (
        P(("rep", "tract"), "head", None),
        P(("rep", "tract")),
        P(("rep", "tract"), None),
        P(None, None, "head"),
        P("head", None),
        P(),
    )
    return jax.shard_map(
        body,
        mesh=mesh,
        in_specs=placed,
        out_specs=P(("rep", "tract"), "head", None),
        check_vma=False,
    )
```

```python
import functools

import jax
import jax.numpy as jnp
from jax import lax
from jax.experimental import pallas as pl
from jax.experimental.pallas import tpu as pltpu
from jax.sharding import PartitionSpec as P

HD = 128
GRANT = 60 * 1024 * 1024
MESH = pl.DeviceIdType.MESH


def meet(n, me, tracts, tract, others):
    barrier = pltpu.get_barrier_semaphore()
    for other in (lax.rem(me + 1, n), lax.rem(me + n - 1, n)):
        pl.semaphore_signal(barrier, inc=1, device_id={"head": other}, device_id_type=MESH)
    for ahead in range(1, tracts):
        other = lax.rem(tract + ahead, tracts)
        pl.semaphore_signal(barrier, inc=1, device_id={"tract": other}, device_id_type=MESH)
    for other in others:
        pl.semaphore_signal(barrier, inc=1, device_id=other, device_id_type=MESH)
    pl.semaphore_wait(barrier, 1 + tracts + len(others))


def sublayer_kernel(
    n,
    tracts,
    reps,
    pieces,
    halves,
    x_ref,
    level_ref,
    visible_ref,
    w_hbm,
    out_hbm,
    table_ref,
    out_ref,
    got,
    wq_ref,
    w_ref,
    q_ref,
    kv_ref,
    kv_in,
    att_ref,
    peak_ref,
    sum_ref,
    acc_ref,
    going,
    landed,
    total_ref,
    load_sem,
    g_send,
    g_recv,
    kv_send,
    kv_recv,
    s_send,
    s_recv,
    w_far,
    att_far,
    f_send,
    f_recv,
):
    me, tract = lax.axis_index("head"), lax.axis_index("tract")
    own = pltpu.make_async_copy(x_ref.at[0], got.at[me], load_sem.at[0])
    own.start()
    load = pltpu.make_async_copy(w_hbm, wq_ref, load_sem.at[1])
    load.start()
    load_out = pltpu.make_async_copy(out_hbm, w_ref, load_sem.at[2])
    load_out.start()
    core, wide = tract % 2, tracts // 2
    chips = wide * reps
    chip = lax.axis_index("rep") * wide + tract // 2
    slab = w_ref.shape[0] // (2 * chips)
    helper = (me == 1) | (me == n - 2)
    ends = (me == 0) | (me == n - 1)

    def seat(by):
        other = lax.rem(chip + by, chips)
        return {"rep": other // wide, "tract": lax.rem(other, wide) * 2 + core}

    def slab_of(which, side):
        start = pl.multiple_of((which * 2 + side) * slab, slab)
        return pl.ds(start, slab)

    def far_copy(kind, span, target, source=None):
        return pltpu.make_async_remote_copy(
            src_ref=(w_far if source is None else source).at[span],
            dst_ref=w_far.at[span],
            send_sem=f_send.at[kind],
            recv_sem=f_recv.at[kind],
            device_id=target,
            device_id_type=MESH,
        )

    inward = {"head": jnp.where(me == 0, 1, n - 2)}
    partner = {"tract": tract + 1 - 2 * core}
    mine = slab_of(chip, core)

    def to_helper():
        return far_copy(0, mine, inward, out_hbm)

    def to_chip(by):
        return far_copy(by, mine, seat(by))

    def from_chip(by):
        return far_copy(by, slab_of(lax.rem(chip + chips - by, chips), core), seat(by))

    def to_partner(by):
        span = slab_of(lax.rem(chip + chips - by, chips), core)
        return far_copy(chips + by, span, partner)

    def from_partner(by):
        span = slab_of(lax.rem(chip + chips - by, chips), 1 - core)
        return far_copy(chips + by, span, partner)

    def att_copy():
        return pltpu.make_async_remote_copy(
            src_ref=att_ref,
            dst_ref=att_far,
            send_sem=f_send.at[2 * chips],
            recv_sem=f_recv.at[2 * chips],
            device_id=inward,
            device_id_type=MESH,
        )

    meet(n, me, tracts, tract, [seat(by) for by in range(1, chips)])
    level = level_ref[0]

    def style(kind):
        return table_ref[kind, pl.ds(level, 1), :]

    rows, width = x_ref.shape[1:]
    part = rows // pieces

    def copy(way, step, piece, first=False):
        side = (way + 1) // 2
        span = pl.ds(piece * part, part)
        block = me - way * step
        return pltpu.make_async_remote_copy(
            src_ref=(x_ref.at[0] if first else got.at[block]).at[span],
            dst_ref=got.at[block].at[span],
            send_sem=g_send.at[side, step, piece],
            recv_sem=g_recv.at[side, step, piece],
            device_id={"head": me + way},
            device_id_type=MESH,
        )

    def arrival(way, step, piece):
        side = (way + 1) // 2
        span = pl.ds(piece * part, part)
        return pltpu.make_async_remote_copy(
            src_ref=x_ref.at[0].at[span],
            dst_ref=got.at[me - way * (step + 1)].at[span],
            send_sem=g_send.at[side, step, piece],
            recv_sem=g_recv.at[side, step, piece],
            device_id={"head": me - way},
            device_id_type=MESH,
        )

    def sends(way, step):
        block, target = me - way * step, me + way
        return (block >= 0) & (block < n) & (target >= 0) & (target < n) & (step < n - 1)

    def receives(way, step):
        block = me - way * (step + 1)
        return (block >= 0) & (block < n)

    def kv_copy(ahead, block):
        return pltpu.make_async_remote_copy(
            src_ref=kv_ref.at[block],
            dst_ref=kv_in.at[ahead - 1, block],
            send_sem=kv_send.at[ahead - 1, block],
            recv_sem=kv_recv.at[ahead - 1, block],
            device_id={"tract": tract + ahead},
            device_id_type=MESH,
        )

    def project(block):
        tokens = got[block].astype(jnp.float32)
        power = jnp.mean(tokens * tokens, axis=-1, keepdims=True)
        normed = tokens * lax.rsqrt(power + 1e-06)
        shaped = (normed * (1.0 + style(1)) + style(0)).astype(jnp.bfloat16)
        for kind in (1, 2, 0):
            made = jnp.dot(shaped, wq_ref[kind], preferred_element_type=jnp.float32)
            made = made.astype(jnp.bfloat16)
            if kind == 0:
                q_ref[block] = made
            else:
                kv_ref[block, kind - 1] = made
            if kind == 2:
                for ahead in range(1, tracts):

                    @pl.when(tract + ahead < tracts)
                    def _():
                        kv_copy(ahead, block).start()

    for piece in range(pieces):
        for way in (-1, 1):

            @pl.when(sends(way, 0))
            def _():
                copy(way, 0, piece, True).start()

    @pl.when(ends)
    def _():
        to_helper().start()

    own.wait()
    load.wait()
    project(me)

    @pl.loop(0, n - 1)
    def _(step):
        for piece in range(pieces):
            for way in (-1, 1):

                @pl.when(receives(way, step))
                def _():
                    arrival(way, step, piece).wait_recv()

                @pl.when(sends(way, step + 1))
                def _():
                    copy(way, step + 1, piece).start()

        @pl.loop(0, 2)
        def _(side):
            way = 2 * side - 1

            @pl.when(receives(way, step))
            def _():
                project(me - way * (step + 1))

        @pl.when(helper & (step == 0))
        def _():
            to_helper().wait_recv()
            for by in range(1, chips):
                to_chip(by).start()
            to_partner(0).start()

    @pl.when(helper)
    def _():
        for by in range(1, chips):
            from_chip(by).wait_recv()
            to_partner(by).start()

    tokens_here = n * rows
    heads_here = q_ref.shape[2] // HD
    scale = HD ** (-0.5)

    def attend(source, allowed):
        for head in range(heads_here):
            lanes = slice(head * HD, (head + 1) * HD)
            queries = q_ref[:, :, lanes].reshape(tokens_here, HD)
            keys = source[:, 0, :, lanes].reshape(tokens_here, HD)
            values = source[:, 1, :, lanes].reshape(tokens_here, HD)
            scores = (
                lax.dot_general(
                    queries, keys, (((1,), (1,)), ((), ())), preferred_element_type=jnp.float32
                )
                * scale
            )
            if allowed is None:
                peak = jnp.max(scores, axis=1, keepdims=True)
                probs = jnp.exp(scores - peak)
            else:
                scores = jnp.where(allowed, scores, -1e30)
                old = peak_ref[head]
                peak = jnp.maximum(old, jnp.max(scores, axis=1, keepdims=True))
                probs = jnp.where(allowed, jnp.exp(scores - peak), 0.0)
                rescale = jnp.exp(old - peak)
            row_sum = jnp.sum(probs, axis=1, keepdims=True)
            weighted = jnp.dot(
                probs.astype(jnp.bfloat16), values, preferred_element_type=jnp.float32
            )
            if allowed is not None:
                row_sum += sum_ref[head] * rescale
                weighted += acc_ref[head] * rescale
            peak_ref[head] = peak
            sum_ref[head] = row_sum
            acc_ref[head] = weighted

    attend(kv_ref, None)
    for ahead in range(1, tracts):

        @pl.when(tract >= ahead)
        def _():
            @pl.loop(0, n)
            def _(block):
                kv_copy(ahead, block).wait_recv()

            attend(kv_in.at[ahead - 1], visible_ref[0, lax.max(tract - ahead, 0)] > 0)

    for head in range(heads_here):
        attended = (acc_ref[head] / sum_ref[head]).astype(jnp.bfloat16)
        att_ref[:, :, head * HD : (head + 1) * HD] = attended.reshape(n, rows, HD)

    @pl.when(ends)
    def _():
        att_copy().start()

    load_out.wait()

    @pl.when(helper)
    def _():
        for by in range(chips):
            from_partner(by).wait_recv()
        att_copy().wait_recv()

    cols = width // halves

    def sum_copy(way, step, piece):
        side = (way + 1) // 2
        span = pl.ds(piece * cols, cols)
        return pltpu.make_async_remote_copy(
            src_ref=going.at[side, step].at[:, span],
            dst_ref=landed.at[side, step].at[:, span],
            send_sem=s_send.at[side, step, piece],
            recv_sem=s_recv.at[side, step, piece],
            device_id={"head": me + way},
            device_id_type=MESH,
        )

    def product(block, piece):
        return jnp.dot(
            att_ref[block],
            w_ref[:, piece * cols : (piece + 1) * cols],
            preferred_element_type=jnp.float32,
        )

    def far_product(block, piece):
        return jnp.dot(
            att_far[block],
            w_far[:, piece * cols : (piece + 1) * cols],
            preferred_element_type=jnp.float32,
        )

    def helps(way):
        return me == (1 if way == 1 else n - 2)

    def owner(way, step):
        return (n - 1 - step) if way == 1 else step

    def sum_sends(way, step):
        block = owner(way, step)
        return (block > me) & (me > 0) if way == 1 else (block < me) & (me < n - 1)

    def sum_receives(way, step):
        block = owner(way, step)
        return (block >= me) & (me > 1) if way == 1 else (block <= me) & (me < n - 2)

    @pl.loop(0, n - 1)
    def _(tick):
        for piece in range(halves):
            span = slice(piece * cols, (piece + 1) * cols)
            for way in (-1, 1):
                side = (way + 1) // 2
                step = tick - (me if way == 1 else n - 1 - me)
                held = (step >= 0) & (step < n - 1)

                @pl.when(held & sum_sends(way, step))
                def _():
                    going[side, step, :, span] = product(owner(way, step), piece).astype(
                        going.dtype
                    )

                    @pl.when(helps(way))
                    def _():
                        going[side, step, :, span] = (
                            going[side, step, :, span].astype(jnp.float32)
                            + far_product(owner(way, step), piece)
                        ).astype(going.dtype)

                    @pl.when(sum_receives(way, step))
                    def _():
                        sum_copy(way, step, piece).wait_recv()
                        going[side, step, :, span] = (
                            going[side, step, :, span].astype(jnp.float32)
                            + landed[side, step, :, span].astype(jnp.float32)
                        ).astype(going.dtype)

                    sum_copy(way, step, piece).start()

    for piece in range(halves):
        span = slice(piece * cols, (piece + 1) * cols)
        total_ref[:, span] = product(me, piece).astype(going.dtype).astype(jnp.float32)
    for piece in range(halves):
        span = slice(piece * cols, (piece + 1) * cols)
        for way in (-1, 1):
            side = (way + 1) // 2
            last = n - 1 - me if way == 1 else me

            @pl.when(helps(way))
            def _():
                total_ref[:, span] += far_product(me, piece)

            @pl.when(me > 1 if way == 1 else me < n - 2)
            def _():
                sum_copy(way, last, piece).wait_recv()
                total_ref[:, span] += landed[side, last, :, span].astype(jnp.float32)

        out_ref[0, :, span] = (
            total_ref[:, span] * table_ref[2, pl.ds(level, 1), span]
        ).astype(out_ref.dtype)

    @pl.loop(0, n - 1)
    def _(step):
        for piece in range(halves):
            for way in (-1, 1):

                @pl.when(sum_sends(way, step))
                def _():
                    sum_copy(way, step, piece).wait_send()

    @pl.loop(0, n)
    def _(block):
        for ahead in range(1, tracts):

            @pl.when(tract + ahead < tracts)
            def _():
                kv_copy(ahead, block).wait_send()

    @pl.loop(0, n - 1)
    def _(step):
        for piece in range(pieces):
            for way in (-1, 1):

                @pl.when(sends(way, step))
                def _():
                    copy(way, step, piece).wait_send()

    @pl.when(ends)
    def _():
        to_helper().wait_send()
        att_copy().wait_send()

    @pl.when(helper)
    def _():
        for by in range(1, chips):
            to_chip(by).wait_send()
        for by in range(chips):
            to_partner(by).wait_send()


def body(frames, levels, visible, w_qkv, w_out, modulation):
    n, tracts = lax.axis_size("head"), lax.axis_size("tract")
    reps = lax.axis_size("rep")
    rows, width = frames.shape[1:]
    cols = w_qkv.shape[2]
    heads_here = cols // HD
    pieces = max(1, rows // 16)
    halves = 4 if width % 512 == 0 else 2
    vmem = pl.BlockSpec(memory_space=pltpu.VMEM)
    hbm = pl.BlockSpec(memory_space=pltpu.HBM)
    smem = pl.BlockSpec(memory_space=pltpu.SMEM)
    half = jnp.bfloat16
    dma = pltpu.SemaphoreType.DMA
    return pl.pallas_call(
        functools.partial(sublayer_kernel, n, tracts, reps, pieces, halves),
        out_shape=jax.ShapeDtypeStruct(frames.shape, frames.dtype),
        in_specs=[hbm, smem, smem, hbm, hbm, vmem],
        out_specs=vmem,
        scratch_shapes=[
            pltpu.VMEM((n, rows, width), half),
            pltpu.VMEM((3, width, cols), half),
            pltpu.VMEM(w_out.shape, half),
            pltpu.VMEM((n, rows, cols), half),
            pltpu.VMEM((n, 2, rows, cols), half),
            pltpu.VMEM((max(1, tracts - 1), n, 2, rows, cols), half),
            pltpu.VMEM((n, rows, cols), half),
            pltpu.VMEM((heads_here, n * rows, 1), jnp.float32),
            pltpu.VMEM((heads_here, n * rows, 1), jnp.float32),
            pltpu.VMEM((heads_here, n * rows, HD), jnp.float32),
            pltpu.VMEM((2, n - 1, rows, width), half),
            pltpu.VMEM((2, n - 1, rows, width), half),
            pltpu.VMEM((rows, width), jnp.float32),
            dma((3,)),
            dma((2, n, pieces)),
            dma((2, n, pieces)),
            dma((tracts, n)),
            dma((tracts, n)),
            dma((2, n, halves)),
            dma((2, n, halves)),
            pltpu.VMEM(w_out.shape, half),
            pltpu.VMEM((n, rows, cols), half),
            dma((tracts * reps + 1,)),
            dma((tracts * reps + 1,)),
        ],
        compiler_params=pltpu.CompilerParams(
            collective_id=0, has_side_effects=True, vmem_limit_bytes=GRANT
        ),
    )(
        frames,
        levels,
        visible,
        jnp.transpose(w_qkv, (1, 0, 2)),
        w_out,
        jnp.transpose(modulation, (1, 0, 2)),
    )


def solution(mesh):
    placed = (
        P(("rep", "tract"), "head", None),
        P(("rep", "tract")),
        P(("rep", "tract"), None),
        P(None, None, "head"),
        P("head", None),
        P(),
    )
    return jax.shard_map(
        body,
        mesh=mesh,
        in_specs=placed,
        out_specs=P(("rep", "tract"), "head", None),
        check_vma=False,
    )
```
